128 devices in a mesh: expert: 32 (over z, y_lo, x), dp: 4 (over y_hi, core).
Axes of the slice: x: 4, y: 4 (y_hi: 2, y_lo: 2; y = y_hi * 2 + y_lo), z: 4, core: 2. Of those that a mesh axis runs over, the one named last changes fastest.
Arguments:
- tokens: bfloat16 [8192, 4096], P(('expert', 'dp')), may hold values from -6 to 6
- expert_ids: int32 [8192, 8], P(('expert', 'dp')), may hold values from 0 to 63, all different within a row; in each aligned block of 64 rows (0 to 63, 64 to 127, ...) at most 10 rows name the same one
- router_weights: float32 [8192, 8], P(('expert', 'dp')), may hold values from 0.1 to 1
- partner: int32 [32], replicated, may hold values from 0 to 31, as said below
- gate_up_weights: bfloat16 [64, 2, 4096, 1024], P('expert', None, None, 'dp'), may hold values from -0.09375 to 0.09375
- down_weights: bfloat16 [64, 1024, 4096], P('expert', 'dp'), may hold values from -0.1875 to 0.1875
Outputs:
- mixed: bfloat16 [8192, 4096], P(('expert', 'dp'))
- arrived_gate_up: bfloat16 [32, 2, 4096, 1024], P('expert', None, None, 'dp')
- arrived_down: bfloat16 [32, 1024, 4096], P('expert', 'dp')
The draws below stay inside these ranges and needn't reach their ends.
Inputs may be any that keep to these rules, and one draw needn't show every extreme that they name: `expert_ids`: at most 10 of the rows of one device name one expert, a bound that some block reaches of a device in every draw; the 8 entries of a row differ. A matching: partner[partner[h]] == h and partner[h] != h for every h.
All inputs are finite; a program needn't handle non-finite values.
Results may differ from the reference program's by a relative error of at most 0.015.
Values may be sent and summed in bfloat16 or wider, within the bound.
No kernel may reach another device: no remote copies, remote signals or barrier semaphores. Data moves between devices by JAX's collectives and lax.ppermute only.
A program may use at most 256 MiB of HBM per device.

```python
import math
import jax
import jax.numpy as jnp
import numpy as np
from jax import lax

D = 4096
FF = 1024
TOP = 8
EXP_DEV = 2
TOK_DEV = 64
HOSTS = 32
EXPERTS = 64
TOKENS = 8192
CAP = 10
N_DP = 4


def draw_partner(key, part):
    order = jax.random.permutation(key, HOSTS).astype(jnp.int32)
    first_half = order[0::2]
    second_half = order[1::2]
    matched = jnp.zeros((HOSTS,), jnp.int32)
    matched = matched.at[first_half].set(second_half)
    return matched.at[second_half].set(first_half)


def level_of(stream_key, extent, shards, smallest, high):
    gain, own = 1.0, jax.random.fold_in(stream_key, 6)
    for axis_at, shards_of in shards:
        steps = jnp.exp(jax.random.uniform(jax.random.fold_in(own, axis_at), (shards_of,), jnp.float32, smallest / len(shards), high / len(shards)))
        gain = gain * jnp.repeat(steps, extent[axis_at] // shards_of).reshape([-1 if axis == axis_at else 1 for axis in range(len(extent))])
    return gain


def shared_out(rng, own, number, rows, number_of, top, most, lean):
    order = jax.random.permutation(rng, number_of)
    crowded, ordinary = load_shares(number_of, rows * top, most, lean, True), load_shares(number_of, rows * top, most, lean, False)
    places = jnp.arange(number_of)

    def named(sizes, offset_by):
        used = int((sizes > 0).sum())
        fixed = max(1, used // 4)
        shifted = fixed + (places - fixed + offset_by * (used - fixed)) % max(1, number_of - fixed)
        return jnp.zeros((number_of,), jnp.int32).at[order[jnp.where(places < fixed, places, shifted)]].set(jnp.asarray(sizes, jnp.int32))

    sizes = jnp.where(number % 4 == 0, named(crowded, number // 4), named(ordinary, number - number // 4 - 1))
    mixed = jax.random.permutation(jax.random.fold_in(own, 3), number_of)
    donor, receiver = mixed[0:number_of // 2 * 2:2], mixed[1:number_of // 2 * 2:2]
    room = jnp.minimum(sizes[donor] - 1, most - sizes[receiver]) // 2
    room = jnp.where((donor == order[0]) | (receiver == order[0]) | (sizes[receiver] == 0), 0, jnp.maximum(room, 0))
    shifted = jax.random.randint(jax.random.fold_in(own, 4), (number_of // 2,), 0, 1 << 20) % (room + 1)
    sizes = sizes.at[donor].add(-shifted).at[receiver].add(shifted)
    items = jnp.searchsorted(jnp.cumsum(sizes), jnp.arange(rows * top), side="right").astype(jnp.int32)
    listing = items.reshape(top, rows).T
    listing = listing[jax.random.permutation(jax.random.fold_in(own, 1), rows)]
    offset_by = jax.random.randint(jax.random.fold_in(own, 2), (rows, 1), 0, top)
    return jnp.take_along_axis(listing, (jnp.arange(top)[None, :] + offset_by) % top, axis=1)


def load_shares(number_of, total, most, slope, full):
    portions = [(1 << 20) // math.isqrt(rank ** slope) + 1 for rank in range(1, number_of + 1)]
    largest = most if full else min(most, max(-(-total // number_of), total * portions[0] // sum(portions)))
    least = 1 if total - largest >= number_of - 1 else 0
    counts, rest = [largest] + [least] * (number_of - 1), total - largest - least * (number_of - 1)
    while rest > 0:
        candidates = [i for i in range(1, number_of) if counts[i] < largest] or [i for i in range(1, number_of) if counts[i] < most]
        mass, remaining = sum([portions[i] for i in candidates]), rest
        for i in candidates:
            extra = min(most - counts[i], max(1, remaining * portions[i] // mass), rest)
            counts[i] = counts[i] + extra
            rest = rest - extra
    return np.array(counts)


def gaussian(own_key, shape, spread, bound, split=(), kind=jnp.bfloat16):
    result = spread * jax.random.normal(own_key, shape, jnp.float32)
    if split:
        result = result * level_of(own_key, shape, split, -0.22, 0.18)
    return jnp.clip(result, -bound, bound).astype(kind)


def setup_inputs(seed: int = 0) -> dict:
    keys = jax.random.split(jax.random.key(seed), 7)
    tokens = gaussian(keys[0], (TOKENS, D), 1.0, 6.0, ((0, 128),))
    expert_ids_keys = jax.random.split(jax.random.fold_in(keys[1], 1), TOKENS // TOK_DEV)
    expert_ids_turns = jax.random.permutation(jax.random.fold_in(keys[1], 3), TOKENS // TOK_DEV)
    expert_ids = jax.vmap(lambda own, number: shared_out(jax.random.fold_in(keys[1], 2), own, number, TOK_DEV, EXPERTS, TOP, CAP, 1))(expert_ids_keys, expert_ids_turns).reshape((TOKENS, TOP))
    router_weights = jnp.clip(jnp.exp(math.log(1.0) - 2.3025851 * jax.random.uniform(keys[2], (TOKENS, TOP), jnp.float32) ** level_of(keys[2], (TOKENS, TOP), ((0, 128),), -0.2, 0.2)), 0.1, 1.0)
    partner = draw_partner(jax.random.fold_in(keys[6], 71), 0)
    gate_up_weights = gaussian(keys[4], (EXPERTS, 2, D, FF), D ** -0.5, 0.09375, ((0, 32), (3, 4)))
    down_weights = gaussian(keys[5], (EXPERTS, FF, D), FF ** -0.5, 0.1875, ((0, 32), (1, 4)))
    return dict(tokens=tokens, expert_ids=expert_ids, router_weights=router_weights, partner=partner, gate_up_weights=gate_up_weights, down_weights=down_weights)


def expert_rows(row_block, gate_up, down_proj):
    gate_value = jnp.dot(row_block, gate_up[0], preferred_element_type=jnp.float32)
    up_value = jnp.dot(row_block, gate_up[1], preferred_element_type=jnp.float32)
    hidden = (jax.nn.silu(gate_value) * up_value).astype(jnp.bfloat16)
    slice_size = hidden.shape[1] // N_DP
    running = jnp.zeros((row_block.shape[0], down_proj.shape[1]), jnp.float32)
    for part_index in range(N_DP):
        offset = part_index * slice_size
        partial_sum = jnp.dot(hidden[:, offset:offset + slice_size], down_proj[offset:offset + slice_size], preferred_element_type=jnp.float32).astype(jnp.bfloat16)
        running = running + partial_sum.astype(jnp.float32)
    return running.astype(jnp.bfloat16)


def reference(tokens, expert_ids, router_weights, partner, gate_up_weights, down_weights):
    device_total = TOKENS // TOK_DEV
    per_device = TOK_DEV * TOP
    ids_block = expert_ids.reshape(device_total, per_device)
    onehot = (ids_block[:, :, None] == jnp.arange(EXPERTS, dtype=jnp.int32)[None, None, :]).astype(jnp.int32)
    slot_index = jnp.sum(jnp.cumsum(onehot, axis=1) * onehot, axis=2) - 1
    device_index = jnp.arange(device_total, dtype=jnp.int32)[:, None]
    column = (device_index * CAP + slot_index).astype(jnp.int32)
    token_index = jnp.repeat(jnp.arange(TOKENS, dtype=jnp.int32).reshape(device_total, TOK_DEV), TOP, axis=1)
    row_table = jnp.full((EXPERTS, device_total * CAP), TOKENS, jnp.int32)
    row_table = row_table.at[ids_block.reshape(-1), column.reshape(-1)].set(token_index.reshape(-1))
    padded = jnp.concatenate([tokens, jnp.zeros((1, D), tokens.dtype)], axis=0)

    def one_expert(operands):
        rows_index, gate_up, down_proj = operands
        return expert_rows(jnp.take(padded, rows_index, axis=0), gate_up, down_proj)

    outputs = lax.map(one_expert, (row_table, gate_up_weights, down_weights))
    flat_out = outputs.reshape(-1, D)
    where_rows = (ids_block * (device_total * CAP) + column).astype(jnp.int32).reshape(TOKENS, TOP)
    normalized = router_weights / jnp.sum(router_weights, axis=1, keepdims=True)
    running = jnp.zeros((TOKENS, D), jnp.float32)
    for choice_rank in range(TOP):
        picked = jnp.take(flat_out, where_rows[:, choice_rank], axis=0).astype(jnp.float32)
        running = running + normalized[:, choice_rank:choice_rank + 1] * picked
    mixed = running.astype(jnp.bfloat16)
    source_expert = (EXP_DEV * partner + EXP_DEV - 1).astype(jnp.int32)
    arrived_gate_up = jnp.take(gate_up_weights, source_expert, axis=0)
    arrived_down = jnp.take(down_weights, source_expert, axis=0)
    return (mixed, arrived_gate_up, arrived_down)
```

```python
import functools

import jax
import jax.numpy as jnp
import numpy as np
from jax import lax
from jax.experimental import pallas as pl
from jax.experimental.pallas import tpu as pltpu
from jax.sharding import Mesh
from jax.sharding import PartitionSpec as P

BF = jnp.bfloat16
F32 = jnp.float32
HOST = ("z", "yl", "x")
PLANE = ("z", "x")
COLUMN = ("yl", "yh")
N_COL = 4
N_PLANE = 16
CAP = 10
SWAP = [(0, 1), (1, 0)]


def place(slot, d):
    width = slot.shape[1]
    row = lax.broadcasted_iota(jnp.int32, (N_COL * CAP, width), 0).astype(F32)
    return [slot[i : i + 1, :] == row for i in (d, d + 1)]


def dispatch_kernel(base_ref, tok_ref, meta_ref, out_ref, slot_ref, weight_ref, place_ref):
    n_tok = tok_ref.shape[0]
    block = n_tok // N_COL
    rows = N_COL * CAP

    @pl.when(pl.program_id(0) == 0)
    def _():
        meta = meta_ref[...].astype(F32).T
        at = lax.broadcasted_iota(jnp.int32, (N_PLANE, 1), 0)
        expert = ((at // 4) * 16 + (at % 4) * 2 + base_ref[0]).astype(F32)
        chosen = jnp.zeros((N_PLANE, n_tok), F32)
        weight = jnp.zeros((N_PLANE, n_tok), F32)
        for k in range(8):
            same = meta[k : k + 1, :] == expert
            w = meta[8 + k : 9 + k, :] + meta[16 + k : 17 + k, :]
            chosen = chosen + jnp.where(same, 1.0, 0.0)
            weight = weight + jnp.where(same, w, 0.0)
        before = lax.broadcasted_iota(jnp.int32, (n_tok, n_tok), 0)
        after = lax.broadcasted_iota(jnp.int32, (n_tok, n_tok), 1)
        earlier = (before < after) & (before // block == after // block)
        rank = jnp.dot(
            chosen.astype(BF),
            jnp.where(earlier, 1.0, 0.0).astype(BF),
            preferred_element_type=F32,
        )
        own = (lax.broadcasted_iota(jnp.int32, (N_PLANE, n_tok), 1) // block).astype(F32)
        slot = jnp.where(chosen > 0.5, rank + own * CAP, -1.0)
        slot_ref[...] = slot
        weight_ref[...] = weight
        for d in range(0, N_PLANE, 2):
            pair = [jnp.where(m, 1.0, 0.0) for m in place(slot, d)]
            place_ref[d * rows : (d + 2) * rows, :] = jnp.concatenate(pair, axis=0).astype(BF)

    out_ref[...] = jnp.dot(
        place_ref[...], tok_ref[...], preferred_element_type=F32
    ).astype(BF)


def dispatch(base, gathered, feature):
    n_tok = gathered.shape[0]
    rows = N_PLANE * N_COL * CAP
    steps = 4
    width = feature // steps
    small = jax.ShapeDtypeStruct((N_PLANE, n_tok), F32)
    return pl.pallas_call(
        dispatch_kernel,
        grid=(steps,),
        in_specs=[
            pl.BlockSpec(memory_space=pltpu.SMEM),
            pl.BlockSpec((n_tok, width), lambda i: (0, i)),
            pl.BlockSpec((n_tok, 128), lambda i: (0, feature // 128)),
        ],
        out_specs=[
            pl.BlockSpec((rows, width), lambda i: (0, i)),
            pl.BlockSpec((N_PLANE, n_tok), lambda i: (0, 0)),
            pl.BlockSpec((N_PLANE, n_tok), lambda i: (0, 0)),
        ],
        out_shape=[jax.ShapeDtypeStruct((rows, feature), BF), small, small],
        scratch_shapes=[pltpu.VMEM((rows, n_tok), BF)],
        compiler_params=pltpu.CompilerParams(vmem_limit_bytes=24 << 20),
        cost_estimate=pl.CostEstimate(
            flops=2 * rows * n_tok * feature,
            bytes_accessed=2 * (rows + n_tok) * feature,
            transcendentals=0,
        ),
        name="dispatch",
    )(base, gathered, gathered)


def combine_kernel(slot_ref, weight_ref, back_ref, out_ref, high_ref, low_ref):
    @pl.when(pl.program_id(0) == 0)
    def _():
        slot = slot_ref[...]
        weight = weight_ref[...]
        parts = []
        for d in range(0, N_PLANE, 2):
            for i, m in enumerate(place(slot, d)):
                parts.append(jnp.where(m, weight[d + i : d + i + 1, :], 0.0))
        mix = jnp.concatenate(parts, axis=0).T
        high = mix.astype(BF)
        high_ref[...] = high
        low_ref[...] = (mix - high.astype(F32)).astype(BF)

    back = back_ref[...]
    total = jnp.dot(high_ref[...], back, preferred_element_type=F32)
    total = total + jnp.dot(low_ref[...], back, preferred_element_type=F32)
    out_ref[...] = total.astype(BF)


def combine(slot, weight, back):
    rows, feature = back.shape
    n_tok = slot.shape[1]
    steps = 4
    width = feature // steps
    return pl.pallas_call(
        combine_kernel,
        grid=(steps,),
        in_specs=[
            pl.BlockSpec((N_PLANE, n_tok), lambda i: (0, 0)),
            pl.BlockSpec((N_PLANE, n_tok), lambda i: (0, 0)),
            pl.BlockSpec((rows, width), lambda i: (0, i)),
        ],
        out_specs=pl.BlockSpec((n_tok, width), lambda i: (0, i)),
        out_shape=jax.ShapeDtypeStruct((n_tok, feature), BF),
        scratch_shapes=[pltpu.VMEM((n_tok, rows), BF)] * 2,
        compiler_params=pltpu.CompilerParams(vmem_limit_bytes=24 << 20),
        cost_estimate=pl.CostEstimate(
            flops=4 * rows * n_tok * feature,
            bytes_accessed=2 * (rows + n_tok) * feature,
            transcendentals=0,
        ),
        name="combine",
    )(slot, weight, back)


def gated(x_ref, w_ref, gate_ref, up_ref):
    feature = x_ref.shape[1]
    step = 512
    gate_ref[...] = jnp.zeros_like(gate_ref)
    up_ref[...] = jnp.zeros_like(up_ref)

    @pl.loop(0, feature // step)
    def _(i):
        at = pl.ds(pl.multiple_of(i * step, step), step)
        x = x_ref[:, at]
        gate_ref[...] += jnp.dot(x, w_ref[0, at, :], preferred_element_type=F32)
        up_ref[...] += jnp.dot(x, w_ref[1, at, :], preferred_element_type=F32)

    gate = gate_ref[...]
    return (gate / (1.0 + jnp.exp(-gate)) * up_ref[...]).astype(BF)


def hidden_kernel(x_hbm, a_hbm, b_hbm, out_ref, x_ref, w_ref, gate_ref, up_ref, sems):
    units = w_ref.shape[3]
    copies = [pltpu.make_async_copy(x_hbm, x_ref, sems.at[0])]
    for i, w_hbm in enumerate((a_hbm, b_hbm)):
        copies.append(pltpu.make_async_copy(w_hbm, w_ref.at[i], sems.at[1 + i]))
    for c in copies:
        c.start()
    copies[0].wait()
    for i in range(2):
        copies[1 + i].wait()
        out_ref[:, i * units : (i + 1) * units] = gated(x_ref, w_ref.at[i], gate_ref, up_ref)


def hidden_half(x, first, second):
    rows, feature = x.shape
    units = first.shape[2]
    anywhere = pl.BlockSpec(memory_space=pl.ANY)
    return pl.pallas_call(
        hidden_kernel,
        in_specs=[anywhere] * 3,
        out_specs=pl.BlockSpec(memory_space=pltpu.VMEM),
        out_shape=jax.ShapeDtypeStruct((rows, 2 * units), BF),
        scratch_shapes=[
            pltpu.VMEM((rows, feature), BF),
            pltpu.VMEM((2, 2, feature, units), BF),
            pltpu.VMEM((rows, units), F32),
            pltpu.VMEM((rows, units), F32),
            pltpu.SemaphoreType.DMA((3,)),
        ],
        compiler_params=pltpu.CompilerParams(vmem_limit_bytes=32 << 20),
        cost_estimate=pl.CostEstimate(
            flops=8 * rows * feature * units,
            bytes_accessed=2 * (rows + 4 * units) * feature,
            transcendentals=rows * units * 2,
        ),
        name="hidden_half",
    )(x, first, second)


def rest_kernel(
    x_hbm, a_hbm, b_hbm, half_ref, d0, d1, d2, d3, out_ref, x_ref, w_ref, down_ref, hid_ref, gate_ref, up_ref, sems
):
    units = w_ref.shape[3]
    feature = x_ref.shape[1]
    copies = [pltpu.make_async_copy(x_hbm, x_ref, sems.at[0])]
    for i, w_hbm in enumerate((a_hbm, b_hbm)):
        copies.append(pltpu.make_async_copy(w_hbm, w_ref.at[i], sems.at[1 + i]))
    for i, d_hbm in enumerate((d0, d1, d2, d3)):
        rows = down_ref.at[pl.ds(i * units, units)]
        copies.append(pltpu.make_async_copy(d_hbm, rows, sems.at[3 + i]))
    for c in copies:
        c.start()
    hid_ref[:, : 2 * units] = half_ref[...]
    copies[0].wait()
    for i in range(2):
        copies[1 + i].wait()
        hid_ref[:, (2 + i) * units : (3 + i) * units] = gated(
            x_ref, w_ref.at[i], gate_ref, up_ref
        )
    for c in copies[3:]:
        c.wait()
    step = 512

    @pl.loop(0, feature // step)
    def _(i):
        at = pl.ds(pl.multiple_of(i * step, step), step)
        out_ref[:, at] = jnp.dot(
            hid_ref[...], down_ref[:, at], preferred_element_type=F32
        ).astype(BF)


def rest(x, first, second, half, downs):
    rows, feature = x.shape
    units = first.shape[2]
    anywhere = pl.BlockSpec(memory_space=pl.ANY)
    vmem = pl.BlockSpec(memory_space=pltpu.VMEM)
    return pl.pallas_call(
        rest_kernel,
        in_specs=[anywhere] * 3 + [vmem] + [anywhere] * 4,
        out_specs=vmem,
        out_shape=jax.ShapeDtypeStruct((rows, feature), BF),
        scratch_shapes=[
            pltpu.VMEM((rows, feature), BF),
            pltpu.VMEM((2, 2, feature, units), BF),
            pltpu.VMEM((4 * units, feature), BF),
            pltpu.VMEM((rows, 4 * units), BF),
            pltpu.VMEM((rows, units), F32),
            pltpu.VMEM((rows, units), F32),
            pltpu.SemaphoreType.DMA((7,)),
        ],
        compiler_params=pltpu.CompilerParams(vmem_limit_bytes=48 << 20),
        cost_estimate=pl.CostEstimate(
            flops=16 * rows * feature * units,
            bytes_accessed=2 * (2 * rows + 8 * units) * feature,
            transcendentals=rows * units * 2,
        ),
        name="rest",
    )(x, first, second, half, *downs)


def pick_kernel(partner_ref, up_ref, down_ref, up_out, down_out, sems):
    n = up_ref.shape[0]

    def copies(i):
        j = partner_ref[i]
        return (
            pltpu.make_async_copy(up_ref.at[j], up_out.at[i], sems.at[0, i]),
            pltpu.make_async_copy(down_ref.at[j], down_out.at[i], sems.at[1, i]),
        )

    @pl.loop(0, n)
    def _(i):
        for c in copies(i):
            c.start()

    @pl.loop(0, n)
    def _(i):
        for c in copies(i):
            c.wait()


def pick(partner, up, down):
    anywhere = pl.BlockSpec(memory_space=pl.ANY)
    return pl.pallas_call(
        pick_kernel,
        in_specs=[pl.BlockSpec(memory_space=pltpu.SMEM), anywhere, anywhere],
        out_specs=[anywhere, anywhere],
        out_shape=[jax.ShapeDtypeStruct(a.shape, a.dtype) for a in (up, down)],
        scratch_shapes=[pltpu.SemaphoreType.DMA((2, up.shape[0]))],
        compiler_params=pltpu.CompilerParams(vmem_limit_bytes=4 << 20),
        cost_estimate=pl.CostEstimate(
            flops=0, bytes_accessed=4 * (up.size + down.size), transcendentals=0
        ),
        name="pick",
    )(partner, up, down)


def exchange(x, axis):
    return lax.all_to_all(x, axis, split_axis=0, concat_axis=0, tiled=True)


def per_device(tokens, expert_ids, router_weights, partner, gate_up, down):
    n_tok, feature = tokens.shape
    units = gate_up.shape[3]
    yh = lax.axis_index("yh")
    base = (lax.axis_index("yl") * 8 + yh).astype(jnp.int32).reshape(1)

    norm = router_weights / jnp.sum(router_weights, axis=1, keepdims=True)
    high = lax.reduce_precision(norm, 8, 7)
    meta = jnp.concatenate(
        [expert_ids.astype(F32), high, norm - high, jnp.zeros((n_tok, 104), F32)], axis=1
    )
    packed = jnp.concatenate([tokens, meta.astype(BF)], axis=1)
    gathered = lax.all_gather(packed, COLUMN, axis=0, tiled=True)

    own_up = lax.dynamic_index_in_dim(gate_up, yh, 0, keepdims=False)
    own_down = lax.dynamic_index_in_dim(down, yh, 0, keepdims=False)
    far_up = lax.ppermute(lax.dynamic_index_in_dim(gate_up, 1 - yh, 0, keepdims=False), "yh", SWAP)
    far_down = lax.ppermute(lax.dynamic_index_in_dim(down, 1 - yh, 0, keepdims=False), "yh", SWAP)
    side_up = lax.ppermute(own_up, "c", SWAP)
    side_down = lax.ppermute(own_down, "c", SWAP)
    far_side_up = lax.ppermute(far_up, "c", SWAP)
    far_side_down = lax.ppermute(far_down, "c", SWAP)

    outgoing, slot, weight = dispatch(base, gathered, feature)
    arrived = exchange(outgoing.reshape(N_PLANE, N_COL * CAP, feature), PLANE)
    x = arrived.reshape(N_PLANE * N_COL * CAP, feature)
    half = hidden_half(x, own_up, side_up)
    y = rest(x, far_up, far_side_up, half, (own_down, side_down, far_down, far_side_down))
    back = exchange(y.reshape(N_PLANE, N_COL * CAP, feature), PLANE)
    part = combine(slot, weight, back.reshape(N_PLANE * N_COL * CAP, feature))
    parts = exchange(part.reshape(N_COL, n_tok, feature), COLUMN)
    mixed = jnp.sum(parts.astype(F32), axis=0).astype(BF)

    hosts = partner.shape[0]
    spread_up = exchange(gate_up[1].reshape(hosts, -1, units), HOST)
    spread_down = exchange(down[1].reshape(hosts, -1, feature), HOST)
    forward_up, forward_down = pick(partner, spread_up, spread_down)
    landed_up = exchange(forward_up, HOST)
    landed_down = exchange(forward_down, HOST)
    return (
        mixed,
        landed_up.reshape((1,) + gate_up.shape[1:]),
        landed_down.reshape((1,) + down.shape[1:]),
    )


def solution(mesh):
    fine = Mesh(np.asarray(mesh.devices).reshape(4, 2, 4, 2, 2), ("z", "yl", "x", "yh", "c"))
    dp = ("yh", "c")
    rows = P(HOST + dp, None)
    up = P(HOST, None, None, dp)
    out = P(HOST, dp, None)
    return jax.shard_map(
        per_device,
        mesh=fine,
        in_specs=(rows, rows, rows, P(), up, out),
        out_specs=(rows, up, out),
        check_vma=False,
    )
```

```python
import functools

import jax
import jax.numpy as jnp
import numpy as np
from jax import lax
from jax.experimental import pallas as pl
from jax.experimental.pallas import tpu as pltpu
from jax.sharding import Mesh
from jax.sharding import PartitionSpec as P

BF = jnp.bfloat16
F32 = jnp.float32
HOST = ("z", "yl", "x")
PLANE = ("z", "x")
COLUMN = ("yl", "yh")
N_COL = 4
N_PLANE = 16
CAP = 10
SWAP = [(0, 1), (1, 0)]


def along_y(step):
    def index(y):
        return (y % 2) * 2 + (y // 2) % 2

    return [(index(y), index((y + step) % N_COL)) for y in range(N_COL)]


def place(slot, d):
    width = slot.shape[1]
    row = lax.broadcasted_iota(jnp.int32, (N_COL * CAP, width), 0).astype(F32)
    return [slot[i : i + 1, :] == row for i in (d, d + 1)]


def placement_kernel(base_ref, *refs):
    metas = refs[:N_COL]
    slot_ref, weight_ref, place_ref = refs[N_COL:]
    block = metas[0].shape[0]
    n_tok = block * N_COL
    rows = N_COL * CAP
    meta = jnp.concatenate([m[...].astype(F32) for m in metas], axis=0).T
    at = lax.broadcasted_iota(jnp.int32, (N_PLANE, 1), 0)
    expert = ((at // 4) * 16 + (at % 4) * 2 + base_ref[0]).astype(F32)
    chosen = jnp.zeros((N_PLANE, n_tok), F32)
    weight = jnp.zeros((N_PLANE, n_tok), F32)
    for k in range(8):
        same = meta[k : k + 1, :] == expert
        chosen = chosen + jnp.where(same, 1.0, 0.0)
        share = meta[8 + k : 9 + k, :] + meta[16 + k : 17 + k, :]
        weight = weight + jnp.where(same, share, 0.0)
    before = lax.broadcasted_iota(jnp.int32, (n_tok, n_tok), 0)
    behind = lax.broadcasted_iota(jnp.int32, (n_tok, n_tok), 1)
    earlier = (before < behind) & (before // block == behind // block)
    rank = jnp.dot(
        chosen.astype(BF), jnp.where(earlier, 1.0, 0.0).astype(BF), preferred_element_type=F32
    )
    own = (lax.broadcasted_iota(jnp.int32, (N_PLANE, n_tok), 1) // block).astype(F32)
    slot = jnp.where(chosen > 0.5, rank + own * CAP, -1.0)
    slot_ref[...] = slot
    weight_ref[...] = weight
    for d in range(0, N_PLANE, 2):
        pair = [jnp.where(m, 1.0, 0.0) for m in place(slot, d)]
        place_ref[d * rows : (d + 2) * rows, :] = jnp.concatenate(pair, axis=0).astype(BF)


def placement(base, blocks, feature):
    block = blocks[0].shape[0]
    n_tok = block * N_COL
    rows = N_PLANE * N_COL * CAP
    small = jax.ShapeDtypeStruct((N_PLANE, n_tok), F32)
    spec = pl.BlockSpec((N_PLANE, n_tok), lambda i: (0, 0))
    return pl.pallas_call(
        placement_kernel,
        grid=(1,),
        in_specs=[pl.BlockSpec(memory_space=pltpu.SMEM)]
        + [pl.BlockSpec((block, 128), lambda i: (0, feature // 128))] * N_COL,
        out_specs=[spec, spec, pl.BlockSpec((rows, n_tok), lambda i: (0, 0))],
        out_shape=[small, small, jax.ShapeDtypeStruct((rows, n_tok), BF)],
        compiler_params=pltpu.CompilerParams(vmem_limit_bytes=16 << 20),
        cost_estimate=pl.CostEstimate(
            flops=rows * n_tok * 4, bytes_accessed=4 * rows * n_tok, transcendentals=0
        ),
        name="placement",
    )(base, *blocks)


def dispatch_kernel(place_ref, *refs):
    toks, (out_ref, tok_ref) = refs[:N_COL], refs[N_COL:]
    block = toks[0].shape[0]
    for i, part in enumerate(toks):
        tok_ref[i * block : (i + 1) * block, :] = part[...]
    out_ref[...] = jnp.dot(
        place_ref[...], tok_ref[...], preferred_element_type=F32
    ).astype(BF)


def dispatch(placed, blocks, feature):
    block = blocks[0].shape[0]
    rows, n_tok = placed.shape
    steps = 4
    width = feature // steps
    return pl.pallas_call(
        dispatch_kernel,
        grid=(steps,),
        in_specs=[pl.BlockSpec((rows, n_tok), lambda i: (0, 0))]
        + [pl.BlockSpec((block, width), lambda i: (0, i))] * N_COL,
        out_specs=pl.BlockSpec((rows, width), lambda i: (0, i)),
        out_shape=jax.ShapeDtypeStruct((rows, feature), BF),
        scratch_shapes=[pltpu.VMEM((n_tok, width), BF)],
        compiler_params=pltpu.CompilerParams(vmem_limit_bytes=56 << 20),
        cost_estimate=pl.CostEstimate(
            flops=2 * rows * n_tok * feature,
            bytes_accessed=2 * (rows + n_tok) * feature,
            transcendentals=0,
        ),
        name="dispatch",
    )(placed, *blocks)


def combine_kernel(slot_ref, weight_ref, back_ref, *refs):
    outs, (high_ref, low_ref) = refs[:N_COL], refs[N_COL:]
    block = outs[0].shape[0]

    @pl.when(pl.program_id(0) == 0)
    def _():
        slot = slot_ref[...]
        weight = weight_ref[...]
        parts = []
        for d in range(0, N_PLANE, 2):
            for i, m in enumerate(place(slot, d)):
                parts.append(jnp.where(m, weight[d + i : d + i + 1, :], 0.0))
        mix = jnp.concatenate(parts, axis=0).T
        high = mix.astype(BF)
        high_ref[...] = high
        low_ref[...] = (mix - high.astype(F32)).astype(BF)

    back = back_ref[...]
    total = jnp.dot(high_ref[...], back, preferred_element_type=F32)
    total = total + jnp.dot(low_ref[...], back, preferred_element_type=F32)
    for i, out_ref in enumerate(outs):
        out_ref[...] = total[i * block : (i + 1) * block, :].astype(out_ref.dtype)


def combine(slot, weight, back):
    rows, feature = back.shape
    n_tok = slot.shape[1]
    block = n_tok // N_COL
    steps = 4
    width = feature // steps
    return pl.pallas_call(
        combine_kernel,
        grid=(steps,),
        in_specs=[
            pl.BlockSpec((N_PLANE, n_tok), lambda i: (0, 0)),
            pl.BlockSpec((N_PLANE, n_tok), lambda i: (0, 0)),
            pl.BlockSpec((rows, width), lambda i: (0, i)),
        ],
        out_specs=[pl.BlockSpec((block, width), lambda i: (0, i))] * N_COL,
        out_shape=[jax.ShapeDtypeStruct((block, feature), F32)]
        + [jax.ShapeDtypeStruct((block, feature), BF)] * (N_COL - 1),
        scratch_shapes=[pltpu.VMEM((n_tok, rows), BF)] * 2,
        compiler_params=pltpu.CompilerParams(vmem_limit_bytes=56 << 20),
        cost_estimate=pl.CostEstimate(
            flops=4 * rows * n_tok * feature,
            bytes_accessed=2 * (rows + n_tok) * feature,
            transcendentals=0,
        ),
        name="combine",
    )(slot, weight, back)


def hidden_kernel(x_hbm, a_hbm, b_hbm, c_hbm, d_hbm, out_ref, x_ref, w_ref, gate_ref, up_ref, sems):
    units = w_ref.shape[3]
    weights = (a_hbm, b_hbm, c_hbm, d_hbm)
    half = x_ref.shape[1] // 2
    loads = []
    for i in range(2):
        at = pl.ds(i * half, half)
        loads.append(pltpu.make_async_copy(x_hbm.at[:, at], x_ref.at[:, at], sems.at[i]))
    fills = [
        [
            pltpu.make_async_copy(
                w.at[:, pl.ds(j * half, half)], w_ref.at[i, :, pl.ds(j * half, half)], sems.at[2 + 2 * i + j]
            )
            for j in range(2)
        ]
        for i, w in enumerate(weights)
    ]
    for c in (loads[0], fills[0][0], loads[1], fills[0][1]):
        c.start()
    for f in fills[1:]:
        for c in f:
            c.start()
    for i in range(4):
        for j in range(2):
            if i == 0:
                loads[j].wait()
            fills[i][j].wait()
            at = slice(j * half, (j + 1) * half)
            x = x_ref[:, at]
            gate = jnp.dot(x, w_ref[i, 0, at, :], preferred_element_type=F32)
            up = jnp.dot(x, w_ref[i, 1, at, :], preferred_element_type=F32)
            if j == 0:
                gate_ref[...] = gate
                up_ref[...] = up
        gate = gate + gate_ref[...]
        up = up + up_ref[...]
        hidden = gate / (1.0 + jnp.exp(-gate)) * up
        out_ref[:, i * units : (i + 1) * units] = hidden.astype(BF)


def hidden_all(x, weights):
    rows, feature = x.shape
    units = weights[0].shape[2]
    anywhere = pl.BlockSpec(memory_space=pl.ANY)
    return pl.pallas_call(
        hidden_kernel,
        in_specs=[anywhere] * 5,
        out_specs=pl.BlockSpec(memory_space=pltpu.VMEM),
        out_shape=jax.ShapeDtypeStruct((rows, 4 * units), BF),
        scratch_shapes=[
            pltpu.VMEM((rows, feature), BF),
            pltpu.VMEM((4, 2, feature, units), BF),
            pltpu.VMEM((rows, units), F32),
            pltpu.VMEM((rows, units), F32),
            pltpu.SemaphoreType.DMA((10,)),
        ],
        compiler_params=pltpu.CompilerParams(vmem_limit_bytes=56 << 20),
        cost_estimate=pl.CostEstimate(
            flops=16 * rows * feature * units,
            bytes_accessed=2 * (rows + 8 * units) * feature,
            transcendentals=rows * units * 4,
        ),
        name="hidden_all",
    )(x, *weights)


def down_kernel(hid_ref, d0, d1, d2, d3, out_ref):
    units = d0.shape[0]
    total = jnp.dot(hid_ref[:, :units], d0[...], preferred_element_type=F32)
    for i, d in enumerate((d1, d2, d3)):
        hid = hid_ref[:, (i + 1) * units : (i + 2) * units]
        total = total + jnp.dot(hid, d[...], preferred_element_type=F32)
    out_ref[...] = total.astype(BF)


def down_all(hidden, downs):
    rows, four = hidden.shape
    units, feature = downs[0].shape
    width = 512
    return pl.pallas_call(
        down_kernel,
        grid=(feature // width,),
        in_specs=[pl.BlockSpec((rows, four), lambda i: (0, 0))]
        + [pl.BlockSpec((units, width), lambda i: (0, i))] * 4,
        out_specs=pl.BlockSpec((rows, width), lambda i: (0, i)),
        out_shape=jax.ShapeDtypeStruct((rows, feature), BF),
        compiler_params=pltpu.CompilerParams(vmem_limit_bytes=56 << 20),
        cost_estimate=pl.CostEstimate(
            flops=8 * rows * feature * units,
            bytes_accessed=2 * (rows + 4 * units) * feature,
            transcendentals=0,
        ),
        name="down_all",
    )(hidden, *downs)


def pick_kernel(source_ref, near_ref, far_ref, out_ref, hold_ref, sems):
    n = near_ref.shape[0]

    @pl.loop(0, n)
    def _(i):
        j = source_ref[i]

        @pl.when(j < n)
        def _():
            pltpu.make_async_copy(near_ref.at[j], hold_ref.at[i], sems.at[0, i]).start()

        @pl.when(j >= n)
        def _():
            pltpu.make_async_copy(far_ref.at[j - n], hold_ref.at[i], sems.at[0, i]).start()

    @pl.loop(0, n)
    def _(i):
        pltpu.make_async_copy(near_ref.at[0], hold_ref.at[i], sems.at[0, i]).wait()
        pltpu.make_async_copy(hold_ref.at[i], out_ref.at[i], sems.at[1, i]).start()

    @pl.loop(0, n)
    def _(i):
        pltpu.make_async_copy(hold_ref.at[i], out_ref.at[i], sems.at[1, i]).wait()


def pick(source, near, far):
    anywhere = pl.BlockSpec(memory_space=pl.ANY)
    return pl.pallas_call(
        pick_kernel,
        in_specs=[pl.BlockSpec(memory_space=pltpu.SMEM), anywhere, anywhere],
        out_specs=anywhere,
        out_shape=jax.ShapeDtypeStruct(near.shape, near.dtype),
        scratch_shapes=[
            pltpu.VMEM(near.shape, near.dtype),
            pltpu.SemaphoreType.DMA((2, near.shape[0])),
        ],
        compiler_params=pltpu.CompilerParams(vmem_limit_bytes=56 << 20),
        cost_estimate=pl.CostEstimate(flops=0, bytes_accessed=4 * near.size, transcendentals=0),
        name="pick",
    )(source, near, far)


def cut_kernel(slot_ref, whole_ref, own_ref, other_ref, give_ref, hold_ref, sems):
    last = whole_ref.shape[0] - 1
    mine = slot_ref[0]

    def load(i):
        return pltpu.make_async_copy(whole_ref.at[i], hold_ref.at[i], sems.at[i])

    for i in range(last + 1):
        load(i).start()
    for i in range(last + 1):
        load(i).wait()
    stores = [
        pltpu.make_async_copy(hold_ref.at[1 - mine], other_ref, sems.at[2]),
        pltpu.make_async_copy(hold_ref.at[mine], own_ref, sems.at[3]),
        pltpu.make_async_copy(hold_ref.at[last], give_ref, sems.at[4]),
    ]
    for c in stores:
        c.start()
    for c in stores:
        c.wait()


def cut(mine, whole):
    anywhere = pl.BlockSpec(memory_space=pl.ANY)
    one = jax.ShapeDtypeStruct(whole.shape[1:], whole.dtype)
    return pl.pallas_call(
        cut_kernel,
        in_specs=[pl.BlockSpec(memory_space=pltpu.SMEM), anywhere],
        out_specs=[anywhere] * 3,
        out_shape=[one] * 3,
        scratch_shapes=[
            pltpu.VMEM(whole.shape, whole.dtype),
            pltpu.SemaphoreType.DMA((5,)),
        ],
        compiler_params=pltpu.CompilerParams(vmem_limit_bytes=56 << 20),
        cost_estimate=pl.CostEstimate(flops=0, bytes_accessed=0, transcendentals=0),
        name="cut",
    )(mine, whole)


def after(x, *earlier):
    return lax.optimization_barrier((x, *earlier))[0]


def exchange(x, axis):
    return lax.all_to_all(x, axis, split_axis=0, concat_axis=0, tiled=True)


def per_device(tokens, expert_ids, router_weights, partner, gate_up, down):
    n_tok, feature = tokens.shape
    units = gate_up.shape[3]
    yh = lax.axis_index("yh")
    yl = lax.axis_index("yl")
    base = (yl * 8 + yh).astype(jnp.int32).reshape(1)

    mine = yh.astype(jnp.int32).reshape(1)
    own_up, other_up, give_up = cut(mine, gate_up)
    own_down, other_down, give_down = cut(mine, down)

    norm = router_weights / jnp.sum(router_weights, axis=1, keepdims=True)
    high = lax.reduce_precision(norm, 8, 7)
    meta = jnp.concatenate(
        [expert_ids.astype(F32), high, norm - high, jnp.zeros((n_tok, 104), F32)], axis=1
    )
    packed = jnp.concatenate([tokens, meta.astype(BF)], axis=1)
    packed = after(packed, give_up)
    blocks = [packed] + [lax.ppermute(packed, COLUMN, along_y(k)) for k in (1, 3, 2)]
    slot, weight, placed = placement(base, blocks, feature)

    near_up = exchange(give_up.reshape(N_PLANE, -1, units), PLANE)
    side_up = lax.ppermute(own_up, "c", SWAP)
    side_down = lax.ppermute(own_down, "c", SWAP)
    far_up = lax.ppermute(after(other_up, *blocks[1:]), "yh", SWAP)
    outgoing = dispatch(placed, blocks, feature)
    outgoing = after(outgoing, near_up, other_down, own_down)
    arrived = exchange(outgoing.reshape(N_PLANE, N_COL * CAP, feature), PLANE)
    x = arrived.reshape(N_PLANE * N_COL * CAP, feature)
    far_down = lax.ppermute(after(other_down, far_up), "yh", SWAP)
    far_side_up = lax.ppermute(far_up, "c", SWAP)
    hidden = hidden_all(x, (own_up, side_up, far_up, far_side_up))
    near_down = exchange(after(give_down, arrived).reshape(N_PLANE, -1, feature), PLANE)
    far_down = after(far_down, hidden, near_down)
    far_side_down = lax.ppermute(far_down, "c", SWAP)
    y = down_all(hidden, (own_down, side_down, far_down, far_side_down))
    back = exchange(y.reshape(N_PLANE, N_COL * CAP, feature), PLANE)
    parts = combine(slot, weight, back.reshape(N_PLANE * N_COL * CAP, feature))
    mixed = parts[0]
    for part, k in zip(parts[1:], (3, 1, 2)):
        mixed = mixed + lax.ppermute(part, COLUMN, along_y(k)).astype(F32)
    mixed = mixed.astype(BF)

    from_host = lax.dynamic_index_in_dim(partner.reshape(4, 2, 4), yl, 1, keepdims=False).reshape(-1)
    crossed = (from_host // 4) % 2 != yl
    source = (from_host // 8) * 4 + from_host % 4 + jnp.where(crossed, N_PLANE, 0)
    source = source.astype(jnp.int32)
    half = near_up.shape[1] // 2
    landed, last = [back], far_down
    for near in (near_up[:, :half], near_up[:, half:], near_down):
        last = lax.ppermute(after(near, last), "yl", SWAP)
        forward = pick(after(source, *parts) if len(landed) == 3 else source, near, last)
        landed.append(exchange(after(forward, landed[-1]), PLANE))
    landed_up = jnp.concatenate(landed[1:3], axis=1)
    landed_down = landed[3]
    return (
        mixed,
        landed_up.reshape((1,) + gate_up.shape[1:]),
        landed_down.reshape((1,) + down.shape[1:]),
    )


def solution(mesh):
    fine = Mesh(np.asarray(mesh.devices).reshape(4, 2, 4, 2, 2), ("z", "yl", "x", "yh", "c"))
    dp = ("yh", "c")
    rows = P(HOST + dp, None)
    up = P(HOST, None, None, dp)
    out = P(HOST, dp, None)
    return jax.shard_map(
        per_device,
        mesh=fine,
        in_specs=(rows, rows, rows, P(), up, out),
        out_specs=(rows, up, out),
        check_vma=False,
    )
```

```python
import functools

import jax
import jax.numpy as jnp
import numpy as np
from jax import lax
from jax.experimental import pallas as pl
from jax.experimental.pallas import tpu as pltpu
from jax.sharding import Mesh
from jax.sharding import PartitionSpec as P

BF = jnp.bfloat16
F32 = jnp.float32
HOST = ("z", "yl", "x")
PLANE = ("z", "x")
COLUMN = ("yl", "yh")
N_COL = 4
N_PLANE = 16
CAP = 10
SWAP = [(0, 1), (1, 0)]


def along_y(step):
    def index(y):
        return (y % 2) * 2 + (y // 2) % 2

    return [(index(y), index((y + step) % N_COL)) for y in range(N_COL)]


def place(slot, d):
    width = slot.shape[1]
    row = lax.broadcasted_iota(jnp.int32, (N_COL * CAP, width), 0).astype(F32)
    return [slot[i : i + 1, :] == row for i in (d, d + 1)]


def placement_kernel(base_ref, *refs):
    metas = refs[:N_COL]
    slot_ref, weight_ref, place_ref = refs[N_COL:]
    block = metas[0].shape[0]
    n_tok = block * N_COL
    rows = N_COL * CAP
    meta = jnp.concatenate([m[...].astype(F32) for m in metas], axis=0).T
    at = lax.broadcasted_iota(jnp.int32, (N_PLANE, 1), 0)
    expert = ((at // 4) * 16 + (at % 4) * 2 + base_ref[0]).astype(F32)
    chosen = jnp.zeros((N_PLANE, n_tok), F32)
    weight = jnp.zeros((N_PLANE, n_tok), F32)
    for k in range(8):
        same = meta[k : k + 1, :] == expert
        chosen = chosen + jnp.where(same, 1.0, 0.0)
        share = meta[8 + k : 9 + k, :] + meta[16 + k : 17 + k, :]
        weight = weight + jnp.where(same, share, 0.0)
    before = lax.broadcasted_iota(jnp.int32, (n_tok, n_tok), 0)
    behind = lax.broadcasted_iota(jnp.int32, (n_tok, n_tok), 1)
    earlier = (before < behind) & (before // block == behind // block)
    rank = jnp.dot(
        chosen.astype(BF), jnp.where(earlier, 1.0, 0.0).astype(BF), preferred_element_type=F32
    )
    own = (lax.broadcasted_iota(jnp.int32, (N_PLANE, n_tok), 1) // block).astype(F32)
    slot = jnp.where(chosen > 0.5, rank + own * CAP, -1.0)
    slot_ref[...] = slot
    weight_ref[...] = weight
    for d in range(0, N_PLANE, 2):
        pair = [jnp.where(m, 1.0, 0.0) for m in place(slot, d)]
        place_ref[d * rows : (d + 2) * rows, :] = jnp.concatenate(pair, axis=0).astype(BF)


def placement(base, blocks, feature):
    block = blocks[0].shape[0]
    n_tok = block * N_COL
    rows = N_PLANE * N_COL * CAP
    small = jax.ShapeDtypeStruct((N_PLANE, n_tok), F32)
    spec = pl.BlockSpec((N_PLANE, n_tok), lambda i: (0, 0))
    return pl.pallas_call(
        placement_kernel,
        grid=(1,),
        in_specs=[pl.BlockSpec(memory_space=pltpu.SMEM)]
        + [pl.BlockSpec((block, 128), lambda i: (0, feature // 128))] * N_COL,
        out_specs=[spec, spec, pl.BlockSpec((rows, n_tok), lambda i: (0, 0))],
        out_shape=[small, small, jax.ShapeDtypeStruct((rows, n_tok), BF)],
        compiler_params=pltpu.CompilerParams(vmem_limit_bytes=16 << 20),
        cost_estimate=pl.CostEstimate(
            flops=rows * n_tok * 4, bytes_accessed=4 * rows * n_tok, transcendentals=0
        ),
        name="placement",
    )(base, *blocks)


def dispatch_kernel(place_ref, *refs):
    toks, (out_ref, tok_ref) = refs[:N_COL], refs[N_COL:]
    block = toks[0].shape[0]
    for i, part in enumerate(toks):
        tok_ref[i * block : (i + 1) * block, :] = part[...]
    out_ref[...] = jnp.dot(
        place_ref[...], tok_ref[...], preferred_element_type=F32
    ).astype(BF)


def dispatch(placed, blocks, feature):
    block = blocks[0].shape[0]
    rows, n_tok = placed.shape
    steps = 4
    width = feature // steps
    return pl.pallas_call(
        dispatch_kernel,
        grid=(steps,),
        in_specs=[pl.BlockSpec((rows, n_tok), lambda i: (0, 0))]
        + [pl.BlockSpec((block, width), lambda i: (0, i))] * N_COL,
        out_specs=pl.BlockSpec((rows, width), lambda i: (0, i)),
        out_shape=jax.ShapeDtypeStruct((rows, feature), BF),
        scratch_shapes=[pltpu.VMEM((n_tok, width), BF)],
        compiler_params=pltpu.CompilerParams(vmem_limit_bytes=56 << 20),
        cost_estimate=pl.CostEstimate(
            flops=2 * rows * n_tok * feature,
            bytes_accessed=2 * (rows + n_tok) * feature,
            transcendentals=0,
        ),
        name="dispatch",
    )(placed, *blocks)


def combine_kernel(slot_ref, weight_ref, back_ref, *refs):
    outs, (high_ref, low_ref) = refs[:N_COL], refs[N_COL:]
    block = outs[0].shape[0]

    @pl.when(pl.program_id(0) == 0)
    def _():
        slot = slot_ref[...]
        weight = weight_ref[...]
        parts = []
        for d in range(0, N_PLANE, 2):
            for i, m in enumerate(place(slot, d)):
                parts.append(jnp.where(m, weight[d + i : d + i + 1, :], 0.0))
        mix = jnp.concatenate(parts, axis=0).T
        high = mix.astype(BF)
        high_ref[...] = high
        low_ref[...] = (mix - high.astype(F32)).astype(BF)

    back = back_ref[...]
    total = jnp.dot(high_ref[...], back, preferred_element_type=F32)
    total = total + jnp.dot(low_ref[...], back, preferred_element_type=F32)
    for i, out_ref in enumerate(outs):
        out_ref[...] = total[i * block : (i + 1) * block, :].astype(out_ref.dtype)


def combine(slot, weight, back):
    rows, feature = back.shape
    n_tok = slot.shape[1]
    block = n_tok // N_COL
    steps = 4
    width = feature // steps
    return pl.pallas_call(
        combine_kernel,
        grid=(steps,),
        in_specs=[
            pl.BlockSpec((N_PLANE, n_tok), lambda i: (0, 0)),
            pl.BlockSpec((N_PLANE, n_tok), lambda i: (0, 0)),
            pl.BlockSpec((rows, width), lambda i: (0, i)),
        ],
        out_specs=[pl.BlockSpec((block, width), lambda i: (0, i))] * N_COL,
        out_shape=[jax.ShapeDtypeStruct((block, feature), F32)]
        + [jax.ShapeDtypeStruct((block, feature), BF)] * (N_COL - 1),
        scratch_shapes=[pltpu.VMEM((n_tok, rows), BF)] * 2,
        compiler_params=pltpu.CompilerParams(vmem_limit_bytes=56 << 20),
        cost_estimate=pl.CostEstimate(
            flops=4 * rows * n_tok * feature,
            bytes_accessed=2 * (rows + n_tok) * feature,
            transcendentals=0,
        ),
        name="combine",
    )(slot, weight, back)


def hidden_kernel(x_hbm, a_hbm, b_hbm, c_hbm, d_hbm, out_ref, x_ref, w_ref, gate_ref, up_ref, sems):
    units = w_ref.shape[3]
    weights = (a_hbm, b_hbm, c_hbm, d_hbm)
    half = x_ref.shape[1] // 2
    loads = []
    for i in range(2):
        at = pl.ds(i * half, half)
        loads.append(pltpu.make_async_copy(x_hbm.at[:, at], x_ref.at[:, at], sems.at[i]))
    fills = [
        [
            pltpu.make_async_copy(
                w.at[:, pl.ds(j * half, half)], w_ref.at[i, :, pl.ds(j * half, half)], sems.at[2 + 2 * i + j]
            )
            for j in range(2)
        ]
        for i, w in enumerate(weights)
    ]
    for c in (loads[0], fills[0][0], loads[1], fills[0][1]):
        c.start()
    for f in fills[1:]:
        for c in f:
            c.start()
    for i in range(4):
        for j in range(2):
            if i == 0:
                loads[j].wait()
            fills[i][j].wait()
            at = slice(j * half, (j + 1) * half)
            x = x_ref[:, at]
            gate = jnp.dot(x, w_ref[i, 0, at, :], preferred_element_type=F32)
            up = jnp.dot(x, w_ref[i, 1, at, :], preferred_element_type=F32)
            if j == 0:
                gate_ref[...] = gate
                up_ref[...] = up
        gate = gate + gate_ref[...]
        up = up + up_ref[...]
        hidden = gate / (1.0 + jnp.exp(-gate)) * up
        out_ref[:, i * units : (i + 1) * units] = hidden.astype(BF)


def hidden_all(x, weights):
    rows, feature = x.shape
    units = weights[0].shape[2]
    anywhere = pl.BlockSpec(memory_space=pl.ANY)
    return pl.pallas_call(
        hidden_kernel,
        in_specs=[anywhere] * 5,
        out_specs=pl.BlockSpec(memory_space=pltpu.VMEM),
        out_shape=jax.ShapeDtypeStruct((rows, 4 * units), BF),
        scratch_shapes=[
            pltpu.VMEM((rows, feature), BF),
            pltpu.VMEM((4, 2, feature, units), BF),
            pltpu.VMEM((rows, units), F32),
            pltpu.VMEM((rows, units), F32),
            pltpu.SemaphoreType.DMA((10,)),
        ],
        compiler_params=pltpu.CompilerParams(vmem_limit_bytes=56 << 20),
        cost_estimate=pl.CostEstimate(
            flops=16 * rows * feature * units,
            bytes_accessed=2 * (rows + 8 * units) * feature,
            transcendentals=rows * units * 4,
        ),
        name="hidden_all",
    )(x, *weights)


def down_kernel(hid_ref, d0, d1, d2, d3, out_ref):
    units = d0.shape[0]
    total = jnp.dot(hid_ref[:, :units], d0[...], preferred_element_type=F32)
    for i, d in enumerate((d1, d2, d3)):
        hid = hid_ref[:, (i + 1) * units : (i + 2) * units]
        total = total + jnp.dot(hid, d[...], preferred_element_type=F32)
    out_ref[...] = total.astype(BF)


def down_all(hidden, downs):
    rows, four = hidden.shape
    units, feature = downs[0].shape
    width = 512
    return pl.pallas_call(
        down_kernel,
        grid=(feature // width,),
        in_specs=[pl.BlockSpec((rows, four), lambda i: (0, 0))]
        + [pl.BlockSpec((units, width), lambda i: (0, i))] * 4,
        out_specs=pl.BlockSpec((rows, width), lambda i: (0, i)),
        out_shape=jax.ShapeDtypeStruct((rows, feature), BF),
        compiler_params=pltpu.CompilerParams(vmem_limit_bytes=56 << 20),
        cost_estimate=pl.CostEstimate(
            flops=8 * rows * feature * units,
            bytes_accessed=2 * (rows + 4 * units) * feature,
            transcendentals=0,
        ),
        name="down_all",
    )(hidden, *downs)


def pick_kernel(source_ref, near_ref, far_ref, out_ref, hold_ref, sems):
    n = near_ref.shape[0]

    @pl.loop(0, n)
    def _(i):
        j = source_ref[i]

        @pl.when(j < n)
        def _():
            pltpu.make_async_copy(near_ref.at[j], hold_ref.at[i], sems.at[0, i]).start()

        @pl.when(j >= n)
        def _():
            pltpu.make_async_copy(far_ref.at[j - n], hold_ref.at[i], sems.at[0, i]).start()

    @pl.loop(0, n)
    def _(i):
        pltpu.make_async_copy(near_ref.at[0], hold_ref.at[i], sems.at[0, i]).wait()
        pltpu.make_async_copy(hold_ref.at[i], out_ref.at[i], sems.at[1, i]).start()

    @pl.loop(0, n)
    def _(i):
        pltpu.make_async_copy(hold_ref.at[i], out_ref.at[i], sems.at[1, i]).wait()


def pick(source, near, far):
    anywhere = pl.BlockSpec(memory_space=pl.ANY)
    return pl.pallas_call(
        pick_kernel,
        in_specs=[pl.BlockSpec(memory_space=pltpu.SMEM), anywhere, anywhere],
        out_specs=anywhere,
        out_shape=jax.ShapeDtypeStruct(near.shape, near.dtype),
        scratch_shapes=[
            pltpu.VMEM(near.shape, near.dtype),
            pltpu.SemaphoreType.DMA((2, near.shape[0])),
        ],
        compiler_params=pltpu.CompilerParams(vmem_limit_bytes=56 << 20),
        cost_estimate=pl.CostEstimate(flops=0, bytes_accessed=4 * near.size, transcendentals=0),
        name="pick",
    )(source, near, far)


def cut_kernel(slot_ref, whole_ref, own_ref, other_ref, hold_ref, sems):
    last = whole_ref.shape[0] - 1
    mine = slot_ref[0]

    def load(i):
        return pltpu.make_async_copy(whole_ref.at[i], hold_ref.at[i], sems.at[i])

    for i in range(last + 1):
        load(i).start()
    for i in range(last + 1):
        load(i).wait()
    stores = [
        pltpu.make_async_copy(hold_ref.at[1 - mine], other_ref, sems.at[2]),
        pltpu.make_async_copy(hold_ref.at[mine], own_ref, sems.at[3]),
    ]
    for c in stores:
        c.start()
    for c in stores:
        c.wait()


def cut(mine, whole):
    anywhere = pl.BlockSpec(memory_space=pl.ANY)
    one = jax.ShapeDtypeStruct(whole.shape[1:], whole.dtype)
    return pl.pallas_call(
        cut_kernel,
        in_specs=[pl.BlockSpec(memory_space=pltpu.SMEM), anywhere],
        out_specs=[anywhere] * 2,
        out_shape=[one] * 2,
        scratch_shapes=[
            pltpu.VMEM(whole.shape, whole.dtype),
            pltpu.SemaphoreType.DMA((4,)),
        ],
        compiler_params=pltpu.CompilerParams(vmem_limit_bytes=56 << 20),
        cost_estimate=pl.CostEstimate(flops=0, bytes_accessed=0, transcendentals=0),
        name="cut",
    )(mine, whole)


def join_kernel(first_ref, second_ref, out_ref, hold_ref, sems):
    rows = first_ref.shape[1]
    loads, stores = [], []
    for i, ref in enumerate((first_ref, second_ref)):
        part = out_ref.at[:, pl.ds(i * rows, rows)]
        loads.append(pltpu.make_async_copy(ref, hold_ref.at[i], sems.at[i]))
        stores.append(pltpu.make_async_copy(hold_ref.at[i], part, sems.at[2 + i]))
    for c in loads:
        c.start()
    for load, store in zip(loads, stores):
        load.wait()
        store.start()
    for c in stores:
        c.wait()


def join(first, second):
    anywhere = pl.BlockSpec(memory_space=pl.ANY)
    n, rows, width = first.shape
    return pl.pallas_call(
        join_kernel,
        in_specs=[anywhere] * 2,
        out_specs=anywhere,
        out_shape=jax.ShapeDtypeStruct((n, 2 * rows, width), first.dtype),
        scratch_shapes=[
            pltpu.VMEM((2, n, rows, width), first.dtype),
            pltpu.SemaphoreType.DMA((4,)),
        ],
        compiler_params=pltpu.CompilerParams(vmem_limit_bytes=56 << 20),
        cost_estimate=pl.CostEstimate(
            flops=0, bytes_accessed=8 * first.size, transcendentals=0
        ),
        name="join",
    )(first, second)


def after(x, *earlier):
    return lax.optimization_barrier((x, *earlier))[0]


def exchange(x, axis):
    return lax.all_to_all(x, axis, split_axis=0, concat_axis=0, tiled=True)


def per_device(tokens, expert_ids, router_weights, partner, gate_up, down):
    n_tok, feature = tokens.shape
    units = gate_up.shape[3]
    yh = lax.axis_index("yh")
    yl = lax.axis_index("yl")
    base = (yl * 8 + yh).astype(jnp.int32).reshape(1)

    mine = yh.astype(jnp.int32).reshape(1)
    give_up, give_down = gate_up[-1], down[-1]
    mine = after(mine, give_up)
    own_up, other_up = cut(mine, gate_up)
    own_down, other_down = cut(mine, down)

    norm = router_weights / jnp.sum(router_weights, axis=1, keepdims=True)
    high = lax.reduce_precision(norm, 8, 7)
    meta = jnp.concatenate(
        [expert_ids.astype(F32), high, norm - high, jnp.zeros((n_tok, 104), F32)], axis=1
    )
    packed = jnp.concatenate([tokens, meta.astype(BF)], axis=1)
    packed = after(packed, give_up)
    blocks = [packed] + [lax.ppermute(packed, COLUMN, along_y(k)) for k in (1, 3, 2)]
    slot, weight, placed = placement(base, blocks, feature)

    near_up = exchange(give_up.reshape(N_PLANE, -1, units), PLANE)
    side_up = lax.ppermute(own_up, "c", SWAP)
    side_down = lax.ppermute(own_down, "c", SWAP)
    far_up = lax.ppermute(after(other_up, *blocks[1:]), "yh", SWAP)
    outgoing = dispatch(placed, blocks, feature)
    outgoing = after(outgoing, near_up, other_down, own_down)
    arrived = exchange(outgoing.reshape(N_PLANE, N_COL * CAP, feature), PLANE)
    x = arrived.reshape(N_PLANE * N_COL * CAP, feature)
    half = near_up.shape[1] // 2
    near_gate, near_rest = near_up[:, :half], near_up[:, half:]
    far_down = lax.ppermute(after(other_down, far_up), "yh", SWAP)
    far_side_up = lax.ppermute(far_up, "c", SWAP)
    hidden = hidden_all(after(x, near_gate, near_rest), (own_up, side_up, far_up, far_side_up))
    near_down = exchange(after(give_down, arrived).reshape(N_PLANE, -1, feature), PLANE)
    far_down = after(far_down, hidden, near_down)
    far_side_down = lax.ppermute(far_down, "c", SWAP)
    y = down_all(hidden, (own_down, side_down, far_down, far_side_down))
    back = exchange(y.reshape(N_PLANE, N_COL * CAP, feature), PLANE)
    parts = combine(slot, weight, back.reshape(N_PLANE * N_COL * CAP, feature))
    from_host = lax.dynamic_index_in_dim(partner.reshape(4, 2, 4), yl, 1, keepdims=False).reshape(-1)
    crossed = (from_host // 4) % 2 != yl
    source = (from_host // 8) * 4 + from_host % 4 + jnp.where(crossed, N_PLANE, 0)
    source = source.astype(jnp.int32)
    nears = (near_gate, near_rest, near_down)
    crossed, last = [], far_down
    for near in nears:
        last = lax.ppermute(after(near, last), "yl", SWAP)
        crossed.append(last)
    landed = [back]
    for i, near in enumerate(nears):
        at = after(source, *(() if i < 2 else parts))
        forward = pick(at, near, crossed[i])
        landed.append(exchange(after(forward, landed[-1]), PLANE))
    landed_up, landed_down = join(landed[1], landed[2]), landed[3]

    mixed = after(parts[0], landed_up)
    for part, k in zip(parts[1:], (3, 1, 2)):
        mixed = mixed + lax.ppermute(part, COLUMN, along_y(k)).astype(F32)
    mixed = mixed.astype(BF)
    return (
        mixed,
        landed_up.reshape((1,) + gate_up.shape[1:]),
        landed_down.reshape((1,) + down.shape[1:]),
    )


def solution(mesh):
    fine = Mesh(np.asarray(mesh.devices).reshape(4, 2, 4, 2, 2), ("z", "yl", "x", "yh", "c"))
    dp = ("yh", "c")
    rows = P(HOST + dp, None)
    up = P(HOST, None, None, dp)
    out = P(HOST, dp, None)
    return jax.shard_map(
        per_device,
        mesh=fine,
        in_specs=(rows, rows, rows, P(), up, out),
        out_specs=(rows, up, out),
        check_vma=False,
    )
```

```python
import functools

import jax
import jax.numpy as jnp
import numpy as np
from jax import lax
from jax.experimental import pallas as pl
from jax.experimental.pallas import tpu as pltpu
from jax.sharding import Mesh
from jax.sharding import PartitionSpec as P

BF = jnp.bfloat16
F32 = jnp.float32
HOST = ("z", "yl", "x")
PLANE = ("x", "z")
COLUMN = ("yl", "yh")
N_COL = 4
N_PLANE = 16
CAP = 10
SWAP = [(0, 1), (1, 0)]


def along_y(step):
    def index(y):
        return (y % 2) * 2 + (y // 2) % 2

    return [(index(y), index((y + step) % N_COL)) for y in range(N_COL)]


def place(slot, d):
    width = slot.shape[1]
    row = lax.broadcasted_iota(jnp.int32, (N_COL * CAP, width), 0).astype(F32)
    return [slot[i : i + 1, :] == row for i in (d, d + 1)]


def placement_kernel(base_ref, *refs):
    metas = refs[:N_COL]
    slot_ref, weight_ref, place_ref = refs[N_COL:]
    block = metas[0].shape[0]
    n_tok = block * N_COL
    rows = N_COL * CAP
    meta = jnp.concatenate([m[...].astype(F32) for m in metas], axis=0).T
    at = lax.broadcasted_iota(jnp.int32, (N_PLANE, 1), 0)
    expert = ((at % 4) * 16 + (at // 4) * 2 + base_ref[0]).astype(F32)
    chosen = jnp.zeros((N_PLANE, n_tok), F32)
    weight = jnp.zeros((N_PLANE, n_tok), F32)
    for k in range(8):
        same = meta[k : k + 1, :] == expert
        chosen = chosen + jnp.where(same, 1.0, 0.0)
        share = meta[8 + k : 9 + k, :] + meta[16 + k : 17 + k, :]
        weight = weight + jnp.where(same, share, 0.0)
    before = lax.broadcasted_iota(jnp.int32, (n_tok, n_tok), 0)
    behind = lax.broadcasted_iota(jnp.int32, (n_tok, n_tok), 1)
    earlier = (before < behind) & (before // block == behind // block)
    rank = jnp.dot(
        chosen.astype(BF), jnp.where(earlier, 1.0, 0.0).astype(BF), preferred_element_type=F32
    )
    own = (lax.broadcasted_iota(jnp.int32, (N_PLANE, n_tok), 1) // block).astype(F32)
    slot = jnp.where(chosen > 0.5, rank + own * CAP, -1.0)
    slot_ref[...] = slot
    weight_ref[...] = weight
    for d in range(0, N_PLANE, 2):
        pair = [jnp.where(m, 1.0, 0.0) for m in place(slot, d)]
        place_ref[d * rows : (d + 2) * rows, :] = jnp.concatenate(pair, axis=0).astype(BF)


def placement(base, blocks, feature):
    block = blocks[0].shape[0]
    n_tok = block * N_COL
    rows = N_PLANE * N_COL * CAP
    small = jax.ShapeDtypeStruct((N_PLANE, n_tok), F32)
    spec = pl.BlockSpec((N_PLANE, n_tok), lambda i: (0, 0))
    return pl.pallas_call(
        placement_kernel,
        grid=(1,),
        in_specs=[pl.BlockSpec(memory_space=pltpu.SMEM)]
        + [pl.BlockSpec((block, 128), lambda i: (0, feature // 128))] * N_COL,
        out_specs=[spec, spec, pl.BlockSpec((rows, n_tok), lambda i: (0, 0))],
        out_shape=[small, small, jax.ShapeDtypeStruct((rows, n_tok), BF)],
        compiler_params=pltpu.CompilerParams(vmem_limit_bytes=16 << 20),
        cost_estimate=pl.CostEstimate(
            flops=rows * n_tok * 4, bytes_accessed=4 * rows * n_tok, transcendentals=0
        ),
        name="placement",
    )(base, *blocks)


def dispatch_kernel(place_ref, *refs):
    toks, (out_ref, tok_ref) = refs[:N_COL], refs[N_COL:]
    block = toks[0].shape[0]
    for i, part in enumerate(toks):
        tok_ref[i * block : (i + 1) * block, :] = part[...]
    out_ref[...] = jnp.dot(
        place_ref[...], tok_ref[...], preferred_element_type=F32
    ).astype(BF)


def dispatch(placed, blocks, feature):
    block = blocks[0].shape[0]
    rows, n_tok = placed.shape
    steps = 4
    width = feature // steps
    return pl.pallas_call(
        dispatch_kernel,
        grid=(steps,),
        in_specs=[pl.BlockSpec((rows, n_tok), lambda i: (0, 0))]
        + [pl.BlockSpec((block, width), lambda i: (0, i))] * N_COL,
        out_specs=pl.BlockSpec((rows, width), lambda i: (0, i)),
        out_shape=jax.ShapeDtypeStruct((rows, feature), BF),
        scratch_shapes=[pltpu.VMEM((n_tok, width), BF)],
        compiler_params=pltpu.CompilerParams(vmem_limit_bytes=56 << 20),
        cost_estimate=pl.CostEstimate(
            flops=2 * rows * n_tok * feature,
            bytes_accessed=2 * (rows + n_tok) * feature,
            transcendentals=0,
        ),
        name="dispatch",
    )(placed, *blocks)


def combine_kernel(slot_ref, weight_ref, back_ref, *refs):
    outs, (high_ref, low_ref) = refs[:N_COL], refs[N_COL:]
    block = outs[0].shape[0]

    @pl.when(pl.program_id(0) == 0)
    def _():
        slot = slot_ref[...]
        weight = weight_ref[...]
        parts = []
        for d in range(0, N_PLANE, 2):
            for i, m in enumerate(place(slot, d)):
                parts.append(jnp.where(m, weight[d + i : d + i + 1, :], 0.0))
        mix = jnp.concatenate(parts, axis=0).T
        high = mix.astype(BF)
        high_ref[...] = high
        low_ref[...] = (mix - high.astype(F32)).astype(BF)

    back = back_ref[...]
    total = jnp.dot(high_ref[...], back, preferred_element_type=F32)
    total = total + jnp.dot(low_ref[...], back, preferred_element_type=F32)
    for i, out_ref in enumerate(outs):
        out_ref[...] = total[i * block : (i + 1) * block, :].astype(out_ref.dtype)


def combine(slot, weight, back):
    rows, feature = back.shape
    n_tok = slot.shape[1]
    block = n_tok // N_COL
    steps = 4
    width = feature // steps
    return pl.pallas_call(
        combine_kernel,
        grid=(steps,),
        in_specs=[
            pl.BlockSpec((N_PLANE, n_tok), lambda i: (0, 0)),
            pl.BlockSpec((N_PLANE, n_tok), lambda i: (0, 0)),
            pl.BlockSpec((rows, width), lambda i: (0, i)),
        ],
        out_specs=[pl.BlockSpec((block, width), lambda i: (0, i))] * N_COL,
        out_shape=[jax.ShapeDtypeStruct((block, feature), F32)]
        + [jax.ShapeDtypeStruct((block, feature), BF)] * (N_COL - 1),
        scratch_shapes=[pltpu.VMEM((n_tok, rows), BF)] * 2,
        compiler_params=pltpu.CompilerParams(vmem_limit_bytes=56 << 20),
        cost_estimate=pl.CostEstimate(
            flops=4 * rows * n_tok * feature,
            bytes_accessed=2 * (rows + n_tok) * feature,
            transcendentals=0,
        ),
        name="combine",
    )(slot, weight, back)


def hidden_kernel(x_hbm, a_hbm, b_hbm, c_hbm, d_hbm, out_ref, x_ref, w_ref, gate_ref, up_ref, sems):
    units = w_ref.shape[3]
    weights = (a_hbm, b_hbm, c_hbm, d_hbm)
    half = x_ref.shape[1] // 2
    loads = []
    for i in range(2):
        at = pl.ds(i * half, half)
        loads.append(pltpu.make_async_copy(x_hbm.at[:, at], x_ref.at[:, at], sems.at[i]))
    fills = [
        [
            pltpu.make_async_copy(
                w.at[:, pl.ds(j * half, half)], w_ref.at[i, :, pl.ds(j * half, half)], sems.at[2 + 2 * i + j]
            )
            for j in range(2)
        ]
        for i, w in enumerate(weights)
    ]
    for c in (loads[0], fills[0][0], loads[1], fills[0][1]):
        c.start()
    for f in fills[1:]:
        for c in f:
            c.start()
    for i in range(4):
        for j in range(2):
            if i == 0:
                loads[j].wait()
            fills[i][j].wait()
            at = slice(j * half, (j + 1) * half)
            x = x_ref[:, at]
            gate = jnp.dot(x, w_ref[i, 0, at, :], preferred_element_type=F32)
            up = jnp.dot(x, w_ref[i, 1, at, :], preferred_element_type=F32)
            if j == 0:
                gate_ref[...] = gate
                up_ref[...] = up
        gate = gate + gate_ref[...]
        up = up + up_ref[...]
        hidden = gate / (1.0 + jnp.exp(-gate)) * up
        out_ref[:, i * units : (i + 1) * units] = hidden.astype(BF)


def hidden_all(x, weights):
    rows, feature = x.shape
    units = weights[0].shape[2]
    anywhere = pl.BlockSpec(memory_space=pl.ANY)
    return pl.pallas_call(
        hidden_kernel,
        in_specs=[anywhere] * 5,
        out_specs=pl.BlockSpec(memory_space=pltpu.VMEM),
        out_shape=jax.ShapeDtypeStruct((rows, 4 * units), BF),
        scratch_shapes=[
            pltpu.VMEM((rows, feature), BF),
            pltpu.VMEM((4, 2, feature, units), BF),
            pltpu.VMEM((rows, units), F32),
            pltpu.VMEM((rows, units), F32),
            pltpu.SemaphoreType.DMA((10,)),
        ],
        compiler_params=pltpu.CompilerParams(vmem_limit_bytes=56 << 20),
        cost_estimate=pl.CostEstimate(
            flops=16 * rows * feature * units,
            bytes_accessed=2 * (rows + 8 * units) * feature,
            transcendentals=rows * units * 4,
        ),
        name="hidden_all",
    )(x, *weights)


def down_kernel(hid_ref, d0, d1, d2, d3, out_ref):
    units = d0.shape[0]
    total = jnp.dot(hid_ref[:, :units], d0[...], preferred_element_type=F32)
    for i, d in enumerate((d1, d2, d3)):
        hid = hid_ref[:, (i + 1) * units : (i + 2) * units]
        total = total + jnp.dot(hid, d[...], preferred_element_type=F32)
    out_ref[...] = total.astype(BF)


def down_all(hidden, downs):
    rows, four = hidden.shape
    units, feature = downs[0].shape
    width = 1024
    return pl.pallas_call(
        down_kernel,
        grid=(feature // width,),
        in_specs=[pl.BlockSpec((rows, four), lambda i: (0, 0))]
        + [pl.BlockSpec((units, width), lambda i: (0, i))] * 4,
        out_specs=pl.BlockSpec((rows, width), lambda i: (0, i)),
        out_shape=jax.ShapeDtypeStruct((rows, feature), BF),
        compiler_params=pltpu.CompilerParams(vmem_limit_bytes=56 << 20),
        cost_estimate=pl.CostEstimate(
            flops=8 * rows * feature * units,
            bytes_accessed=2 * (rows + 4 * units) * feature,
            transcendentals=0,
        ),
        name="down_all",
    )(hidden, *downs)


def pick_kernel(source_ref, near_ref, far_ref, out_ref, hold_ref, sems):
    n = near_ref.shape[0]

    @pl.loop(0, n)
    def _(i):
        j = source_ref[i]

        @pl.when(j < n)
        def _():
            pltpu.make_async_copy(near_ref.at[j], hold_ref.at[i], sems.at[0, i]).start()

        @pl.when(j >= n)
        def _():
            pltpu.make_async_copy(far_ref.at[j - n], hold_ref.at[i], sems.at[0, i]).start()

    @pl.loop(0, n)
    def _(i):
        pltpu.make_async_copy(near_ref.at[0], hold_ref.at[i], sems.at[0, i]).wait()
        pltpu.make_async_copy(hold_ref.at[i], out_ref.at[i], sems.at[1, i]).start()

    @pl.loop(0, n)
    def _(i):
        pltpu.make_async_copy(hold_ref.at[i], out_ref.at[i], sems.at[1, i]).wait()


def pick(source, near, far):
    anywhere = pl.BlockSpec(memory_space=pl.ANY)
    return pl.pallas_call(
        pick_kernel,
        in_specs=[pl.BlockSpec(memory_space=pltpu.SMEM), anywhere, anywhere],
        out_specs=anywhere,
        out_shape=jax.ShapeDtypeStruct(near.shape, near.dtype),
        scratch_shapes=[
            pltpu.VMEM(near.shape, near.dtype),
            pltpu.SemaphoreType.DMA((2, near.shape[0])),
        ],
        compiler_params=pltpu.CompilerParams(vmem_limit_bytes=56 << 20),
        cost_estimate=pl.CostEstimate(flops=0, bytes_accessed=4 * near.size, transcendentals=0),
        name="pick",
    )(source, near, far)


def cut_kernel(slot_ref, whole_ref, own_ref, other_ref, hold_ref, sems):
    last = whole_ref.shape[0] - 1
    mine = slot_ref[0]

    def load(i):
        return pltpu.make_async_copy(whole_ref.at[i], hold_ref.at[i], sems.at[i])

    for i in range(last + 1):
        load(i).start()
    for i in range(last + 1):
        load(i).wait()
    stores = [
        pltpu.make_async_copy(hold_ref.at[1 - mine], other_ref, sems.at[2]),
        pltpu.make_async_copy(hold_ref.at[mine], own_ref, sems.at[3]),
    ]
    for c in stores:
        c.start()
    for c in stores:
        c.wait()


def cut(mine, whole):
    anywhere = pl.BlockSpec(memory_space=pl.ANY)
    one = jax.ShapeDtypeStruct(whole.shape[1:], whole.dtype)
    return pl.pallas_call(
        cut_kernel,
        in_specs=[pl.BlockSpec(memory_space=pltpu.SMEM), anywhere],
        out_specs=[anywhere] * 2,
        out_shape=[one] * 2,
        scratch_shapes=[
            pltpu.VMEM(whole.shape, whole.dtype),
            pltpu.SemaphoreType.DMA((4,)),
        ],
        compiler_params=pltpu.CompilerParams(vmem_limit_bytes=56 << 20),
        cost_estimate=pl.CostEstimate(flops=0, bytes_accessed=0, transcendentals=0),
        name="cut",
    )(mine, whole)


def join_kernel(first_ref, second_ref, out_ref, hold_ref, sems):
    rows = first_ref.shape[1]
    loads, stores = [], []
    for i, ref in enumerate((first_ref, second_ref)):
        part = out_ref.at[:, pl.ds(i * rows, rows)]
        loads.append(pltpu.make_async_copy(ref, hold_ref.at[i], sems.at[i]))
        stores.append(pltpu.make_async_copy(hold_ref.at[i], part, sems.at[2 + i]))
    for c in loads:
        c.start()
    for load, store in zip(loads, stores):
        load.wait()
        store.start()
    for c in stores:
        c.wait()


def join(first, second):
    anywhere = pl.BlockSpec(memory_space=pl.ANY)
    n, rows, width = first.shape
    return pl.pallas_call(
        join_kernel,
        in_specs=[anywhere] * 2,
        out_specs=anywhere,
        out_shape=jax.ShapeDtypeStruct((n, 2 * rows, width), first.dtype),
        scratch_shapes=[
            pltpu.VMEM((2, n, rows, width), first.dtype),
            pltpu.SemaphoreType.DMA((4,)),
        ],
        compiler_params=pltpu.CompilerParams(vmem_limit_bytes=56 << 20),
        cost_estimate=pl.CostEstimate(
            flops=0, bytes_accessed=8 * first.size, transcendentals=0
        ),
        name="join",
    )(first, second)


def after(x, *earlier):
    return lax.optimization_barrier((x, *earlier))[0]


def exchange(x, axis):
    return lax.all_to_all(x, axis, split_axis=0, concat_axis=0, tiled=True)


def per_device(tokens, expert_ids, router_weights, partner, gate_up, down):
    n_tok, feature = tokens.shape
    units = gate_up.shape[3]
    yh = lax.axis_index("yh")
    yl = lax.axis_index("yl")
    base = (yl * 8 + yh).astype(jnp.int32).reshape(1)

    mine = yh.astype(jnp.int32).reshape(1)
    give_up, give_down = gate_up[-1], down[-1]
    mine = after(mine, give_up)
    own_up, other_up = cut(mine, gate_up)
    own_down, other_down = cut(mine, down)

    norm = router_weights / jnp.sum(router_weights, axis=1, keepdims=True)
    high = lax.reduce_precision(norm, 8, 7)
    meta = jnp.concatenate(
        [expert_ids.astype(F32), high, norm - high, jnp.zeros((n_tok, 104), F32)], axis=1
    )
    packed = jnp.concatenate([tokens, meta.astype(BF)], axis=1)
    packed = after(packed, give_up)
    blocks = [packed] + [lax.ppermute(packed, COLUMN, along_y(k)) for k in (1, 3, 2)]
    slot, weight, placed = placement(base, blocks, feature)

    near_up = exchange(give_up.reshape(N_PLANE, -1, units), PLANE)
    side_up = lax.ppermute(own_up, "c", SWAP)
    side_down = lax.ppermute(own_down, "c", SWAP)
    far_up = lax.ppermute(after(other_up, *blocks[1:]), "yh", SWAP)
    outgoing = dispatch(placed, blocks, feature)
    outgoing = after(outgoing, near_up, other_down, own_down)
    arrived = exchange(outgoing.reshape(N_PLANE, N_COL * CAP, feature), PLANE)
    x = arrived.reshape(N_PLANE * N_COL * CAP, feature)
    half = near_up.shape[1] // 2
    near_gate, near_rest = near_up[:, :half], near_up[:, half:]
    far_down = lax.ppermute(after(other_down, far_up), "yh", SWAP)
    far_side_up = lax.ppermute(far_up, "c", SWAP)
    hidden = hidden_all(after(x, near_gate, near_rest), (own_up, side_up, far_up, far_side_up))
    near_down = exchange(after(give_down, arrived).reshape(N_PLANE, -1, feature), PLANE)
    far_down = after(far_down, hidden, near_down)
    far_side_down = lax.ppermute(far_down, "c", SWAP)
    y = down_all(hidden, (own_down, side_down, far_down, far_side_down))
    back = exchange(y.reshape(N_PLANE, N_COL * CAP, feature), PLANE)
    parts = combine(slot, weight, back.reshape(N_PLANE * N_COL * CAP, feature))
    from_host = lax.dynamic_index_in_dim(partner.reshape(4, 2, 4), yl, 1, keepdims=False)
    from_host = from_host.T.reshape(-1)
    crossed = (from_host // 4) % 2 != yl
    source = (from_host % 4) * 4 + from_host // 8 + jnp.where(crossed, N_PLANE, 0)
    source = source.astype(jnp.int32)
    nears = (near_gate, near_rest, near_down)
    crossed, last = [], far_down
    for near in nears:
        last = lax.ppermute(after(near, last), "yl", SWAP)
        crossed.append(last)
    landed = [back]
    for i, near in enumerate(nears):
        at = after(source, *(() if i < 2 else parts))
        forward = pick(at, near, crossed[i])
        landed.append(exchange(after(forward, landed[-1]), PLANE))
    landed_up, landed_down = join(landed[1], landed[2]), landed[3]

    mixed = after(parts[0], landed_up)
    for part, k in zip(parts[1:], (3, 1, 2)):
        mixed = mixed + lax.ppermute(part, COLUMN, along_y(k)).astype(F32)
    mixed = mixed.astype(BF)
    return (
        mixed,
        landed_up.reshape((1,) + gate_up.shape[1:]),
        landed_down.reshape((1,) + down.shape[1:]),
    )


def solution(mesh):
    fine = Mesh(np.asarray(mesh.devices).reshape(4, 2, 4, 2, 2), ("z", "yl", "x", "yh", "c"))
    dp = ("yh", "c")
    rows = P(HOST + dp, None)
    up = P(HOST, None, None, dp)
    out = P(HOST, dp, None)
    return jax.shard_map(
        per_device,
        mesh=fine,
        in_specs=(rows, rows, rows, P(), up, out),
        out_specs=(rows, up, out),
        check_vma=False,
    )
```

```python
import functools

import jax
import jax.numpy as jnp
import numpy as np
from jax import lax
from jax.experimental import pallas as pl
from jax.experimental.pallas import tpu as pltpu
from jax.sharding import Mesh
from jax.sharding import PartitionSpec as P

BF = jnp.bfloat16
F32 = jnp.float32
HOST = ("z", "yl", "x")
PLANE = ("x", "z")
COLUMN = ("yl", "yh")
N_COL = 4
N_PLANE = 16
CAP = 10
SWAP = [(0, 1), (1, 0)]


def along_y(step):
    def index(y):
        return (y % 2) * 2 + (y // 2) % 2

    return [(index(y), index((y + step) % N_COL)) for y in range(N_COL)]


def place(slot, d):
    width = slot.shape[1]
    row = lax.broadcasted_iota(jnp.int32, (N_COL * CAP, width), 0).astype(F32)
    return [slot[i : i + 1, :] == row for i in (d, d + 1)]


def placement_kernel(base_ref, *refs):
    metas = refs[:N_COL]
    slot_ref, weight_ref, place_ref = refs[N_COL:]
    block = metas[0].shape[0]
    n_tok = block * N_COL
    rows = N_COL * CAP
    meta = jnp.concatenate([m[...].astype(F32) for m in metas], axis=0).T
    at = lax.broadcasted_iota(jnp.int32, (N_PLANE, 1), 0)
    expert = ((at % 4) * 16 + (at // 4) * 2 + base_ref[0]).astype(F32)
    chosen = jnp.zeros((N_PLANE, n_tok), F32)
    weight = jnp.zeros((N_PLANE, n_tok), F32)
    for k in range(8):
        same = meta[k : k + 1, :] == expert
        chosen = chosen + jnp.where(same, 1.0, 0.0)
        share = meta[8 + k : 9 + k, :] + meta[16 + k : 17 + k, :]
        weight = weight + jnp.where(same, share, 0.0)
    before = lax.broadcasted_iota(jnp.int32, (n_tok, n_tok), 0)
    behind = lax.broadcasted_iota(jnp.int32, (n_tok, n_tok), 1)
    earlier = (before < behind) & (before // block == behind // block)
    rank = jnp.dot(
        chosen.astype(BF), jnp.where(earlier, 1.0, 0.0).astype(BF), preferred_element_type=F32
    )
    own = (lax.broadcasted_iota(jnp.int32, (N_PLANE, n_tok), 1) // block).astype(F32)
    slot = jnp.where(chosen > 0.5, rank + own * CAP, -1.0)
    slot_ref[...] = slot
    weight_ref[...] = weight
    for d in range(0, N_PLANE, 2):
        pair = [jnp.where(m, 1.0, 0.0) for m in place(slot, d)]
        place_ref[d * rows : (d + 2) * rows, :] = jnp.concatenate(pair, axis=0).astype(BF)


def placement(base, blocks, feature):
    block = blocks[0].shape[0]
    n_tok = block * N_COL
    rows = N_PLANE * N_COL * CAP
    small = jax.ShapeDtypeStruct((N_PLANE, n_tok), F32)
    spec = pl.BlockSpec((N_PLANE, n_tok), lambda i: (0, 0))
    return pl.pallas_call(
        placement_kernel,
        grid=(1,),
        in_specs=[pl.BlockSpec(memory_space=pltpu.SMEM)]
        + [pl.BlockSpec((block, 128), lambda i: (0, feature // 128))] * N_COL,
        out_specs=[spec, spec, pl.BlockSpec((rows, n_tok), lambda i: (0, 0))],
        out_shape=[small, small, jax.ShapeDtypeStruct((rows, n_tok), BF)],
        compiler_params=pltpu.CompilerParams(vmem_limit_bytes=16 << 20),
        cost_estimate=pl.CostEstimate(
            flops=rows * n_tok * 4, bytes_accessed=4 * rows * n_tok, transcendentals=0
        ),
        name="placement",
    )(base, *blocks)


def dispatch_kernel(place_ref, *refs):
    toks, (out_ref, tok_ref) = refs[:N_COL], refs[N_COL:]
    block = toks[0].shape[0]
    for i, part in enumerate(toks):
        tok_ref[i * block : (i + 1) * block, :] = part[...]
    out_ref[...] = jnp.dot(
        place_ref[...], tok_ref[...], preferred_element_type=F32
    ).astype(BF)


def dispatch(placed, blocks, feature):
    block = blocks[0].shape[0]
    rows, n_tok = placed.shape
    steps = 4
    width = feature // steps
    return pl.pallas_call(
        dispatch_kernel,
        grid=(steps,),
        in_specs=[pl.BlockSpec((rows, n_tok), lambda i: (0, 0))]
        + [pl.BlockSpec((block, width), lambda i: (0, i))] * N_COL,
        out_specs=pl.BlockSpec((rows, width), lambda i: (0, i)),
        out_shape=jax.ShapeDtypeStruct((rows, feature), BF),
        scratch_shapes=[pltpu.VMEM((n_tok, width), BF)],
        compiler_params=pltpu.CompilerParams(vmem_limit_bytes=56 << 20),
        cost_estimate=pl.CostEstimate(
            flops=2 * rows * n_tok * feature,
            bytes_accessed=2 * (rows + n_tok) * feature,
            transcendentals=0,
        ),
        name="dispatch",
    )(placed, *blocks)


def combine_kernel(slot_ref, weight_ref, back_ref, *refs):
    outs, (high_ref, low_ref) = refs[:N_COL], refs[N_COL:]
    block = outs[0].shape[0]

    @pl.when(pl.program_id(0) == 0)
    def _():
        slot = slot_ref[...]
        weight = weight_ref[...]
        parts = []
        for d in range(0, N_PLANE, 2):
            for i, m in enumerate(place(slot, d)):
                parts.append(jnp.where(m, weight[d + i : d + i + 1, :], 0.0))
        mix = jnp.concatenate(parts, axis=0).T
        high = mix.astype(BF)
        high_ref[...] = high
        low_ref[...] = (mix - high.astype(F32)).astype(BF)

    back = back_ref[...]
    total = jnp.dot(high_ref[...], back, preferred_element_type=F32)
    total = total + jnp.dot(low_ref[...], back, preferred_element_type=F32)
    for i, out_ref in enumerate(outs):
        out_ref[...] = total[i * block : (i + 1) * block, :].astype(out_ref.dtype)


def combine(slot, weight, back):
    rows, feature = back.shape
    n_tok = slot.shape[1]
    block = n_tok // N_COL
    steps = 4
    width = feature // steps
    return pl.pallas_call(
        combine_kernel,
        grid=(steps,),
        in_specs=[
            pl.BlockSpec((N_PLANE, n_tok), lambda i: (0, 0)),
            pl.BlockSpec((N_PLANE, n_tok), lambda i: (0, 0)),
            pl.BlockSpec((rows, width), lambda i: (0, i)),
        ],
        out_specs=[pl.BlockSpec((block, width), lambda i: (0, i))] * N_COL,
        out_shape=[jax.ShapeDtypeStruct((block, feature), F32)]
        + [jax.ShapeDtypeStruct((block, feature), BF)] * (N_COL - 1),
        scratch_shapes=[pltpu.VMEM((n_tok, rows), BF)] * 2,
        compiler_params=pltpu.CompilerParams(vmem_limit_bytes=56 << 20),
        cost_estimate=pl.CostEstimate(
            flops=4 * rows * n_tok * feature,
            bytes_accessed=2 * (rows + n_tok) * feature,
            transcendentals=0,
        ),
        name="combine",
    )(slot, weight, back)


def hidden_kernel(x_hbm, a_hbm, b_hbm, c_hbm, d_hbm, out_ref, x_ref, w_ref, gate_ref, up_ref, sems):
    units = w_ref.shape[3]
    weights = (a_hbm, b_hbm, c_hbm, d_hbm)
    half = x_ref.shape[1] // 2
    loads = []
    for i in range(2):
        at = pl.ds(i * half, half)
        loads.append(pltpu.make_async_copy(x_hbm.at[:, at], x_ref.at[:, at], sems.at[i]))
    fills = [
        [
            pltpu.make_async_copy(
                w.at[:, pl.ds(j * half, half)], w_ref.at[i, :, pl.ds(j * half, half)], sems.at[2 + 2 * i + j]
            )
            for j in range(2)
        ]
        for i, w in enumerate(weights)
    ]
    for c in (loads[0], fills[0][0], loads[1], fills[0][1]):
        c.start()
    for f in fills[1:]:
        for c in f:
            c.start()
    for i in range(4):
        for j in range(2):
            if i == 0:
                loads[j].wait()
            fills[i][j].wait()
            at = slice(j * half, (j + 1) * half)
            x = x_ref[:, at]
            gate = jnp.dot(x, w_ref[i, 0, at, :], preferred_element_type=F32)
            up = jnp.dot(x, w_ref[i, 1, at, :], preferred_element_type=F32)
            if j == 0:
                gate_ref[...] = gate
                up_ref[...] = up
        gate = gate + gate_ref[...]
        up = up + up_ref[...]
        hidden = gate / (1.0 + jnp.exp(-gate)) * up
        out_ref[:, i * units : (i + 1) * units] = hidden.astype(BF)


def hidden_all(x, weights):
    rows, feature = x.shape
    units = weights[0].shape[2]
    anywhere = pl.BlockSpec(memory_space=pl.ANY)
    return pl.pallas_call(
        hidden_kernel,
        in_specs=[anywhere] * 5,
        out_specs=pl.BlockSpec(memory_space=pltpu.VMEM),
        out_shape=jax.ShapeDtypeStruct((rows, 4 * units), BF),
        scratch_shapes=[
            pltpu.VMEM((rows, feature), BF),
            pltpu.VMEM((4, 2, feature, units), BF),
            pltpu.VMEM((rows, units), F32),
            pltpu.VMEM((rows, units), F32),
            pltpu.SemaphoreType.DMA((10,)),
        ],
        compiler_params=pltpu.CompilerParams(vmem_limit_bytes=56 << 20),
        cost_estimate=pl.CostEstimate(
            flops=16 * rows * feature * units,
            bytes_accessed=2 * (rows + 8 * units) * feature,
            transcendentals=rows * units * 4,
        ),
        name="hidden_all",
    )(x, *weights)


def down_kernel(hid_ref, d0, d1, d2, d3, out_ref):
    units = d0.shape[0]
    total = jnp.dot(hid_ref[:, :units], d0[...], preferred_element_type=F32)
    for i, d in enumerate((d1, d2, d3)):
        hid = hid_ref[:, (i + 1) * units : (i + 2) * units]
        total = total + jnp.dot(hid, d[...], preferred_element_type=F32)
    out_ref[...] = total.astype(BF)


def down_all(hidden, downs):
    rows, four = hidden.shape
    units, feature = downs[0].shape
    width = 2048
    return pl.pallas_call(
        down_kernel,
        grid=(feature // width,),
        in_specs=[pl.BlockSpec((rows, four), lambda i: (0, 0))]
        + [pl.BlockSpec((units, width), lambda i: (0, i))] * 4,
        out_specs=pl.BlockSpec((rows, width), lambda i: (0, i)),
        out_shape=jax.ShapeDtypeStruct((rows, feature), BF),
        compiler_params=pltpu.CompilerParams(vmem_limit_bytes=56 << 20),
        cost_estimate=pl.CostEstimate(
            flops=8 * rows * feature * units,
            bytes_accessed=2 * (rows + 4 * units) * feature,
            transcendentals=0,
        ),
        name="down_all",
    )(hidden, *downs)


def pick_kernel(source_ref, near_ref, far_ref, out_ref, hold_ref, sems):
    n = near_ref.shape[0]

    @pl.loop(0, n)
    def _(i):
        j = source_ref[i]

        @pl.when(j < n)
        def _():
            pltpu.make_async_copy(near_ref.at[j], hold_ref.at[i], sems.at[0, i]).start()

        @pl.when(j >= n)
        def _():
            pltpu.make_async_copy(far_ref.at[j - n], hold_ref.at[i], sems.at[0, i]).start()

    @pl.loop(0, n)
    def _(i):
        pltpu.make_async_copy(near_ref.at[0], hold_ref.at[i], sems.at[0, i]).wait()
        pltpu.make_async_copy(hold_ref.at[i], out_ref.at[i], sems.at[1, i]).start()

    @pl.loop(0, n)
    def _(i):
        pltpu.make_async_copy(hold_ref.at[i], out_ref.at[i], sems.at[1, i]).wait()


def pick(source, near, far):
    anywhere = pl.BlockSpec(memory_space=pl.ANY)
    return pl.pallas_call(
        pick_kernel,
        in_specs=[pl.BlockSpec(memory_space=pltpu.SMEM), anywhere, anywhere],
        out_specs=anywhere,
        out_shape=jax.ShapeDtypeStruct(near.shape, near.dtype),
        scratch_shapes=[
            pltpu.VMEM(near.shape, near.dtype),
            pltpu.SemaphoreType.DMA((2, near.shape[0])),
        ],
        compiler_params=pltpu.CompilerParams(vmem_limit_bytes=56 << 20),
        cost_estimate=pl.CostEstimate(flops=0, bytes_accessed=4 * near.size, transcendentals=0),
        name="pick",
    )(source, near, far)


def cut_kernel(slot_ref, whole_ref, own_ref, other_ref, hold_ref, sems):
    last = whole_ref.shape[0] - 1
    mine = slot_ref[0]

    def load(i):
        return pltpu.make_async_copy(whole_ref.at[i], hold_ref.at[i], sems.at[i])

    for i in range(last + 1):
        load(i).start()
    for i in range(last + 1):
        load(i).wait()
    stores = [
        pltpu.make_async_copy(hold_ref.at[1 - mine], other_ref, sems.at[2]),
        pltpu.make_async_copy(hold_ref.at[mine], own_ref, sems.at[3]),
    ]
    for c in stores:
        c.start()
    for c in stores:
        c.wait()


def cut(mine, whole):
    anywhere = pl.BlockSpec(memory_space=pl.ANY)
    one = jax.ShapeDtypeStruct(whole.shape[1:], whole.dtype)
    return pl.pallas_call(
        cut_kernel,
        in_specs=[pl.BlockSpec(memory_space=pltpu.SMEM), anywhere],
        out_specs=[anywhere] * 2,
        out_shape=[one] * 2,
        scratch_shapes=[
            pltpu.VMEM(whole.shape, whole.dtype),
            pltpu.SemaphoreType.DMA((4,)),
        ],
        compiler_params=pltpu.CompilerParams(vmem_limit_bytes=56 << 20),
        cost_estimate=pl.CostEstimate(flops=0, bytes_accessed=0, transcendentals=0),
        name="cut",
    )(mine, whole)


def join_kernel(first_ref, second_ref, out_ref, hold_ref, sems):
    rows = first_ref.shape[1]
    loads, stores = [], []
    for i, ref in enumerate((first_ref, second_ref)):
        part = out_ref.at[:, pl.ds(i * rows, rows)]
        loads.append(pltpu.make_async_copy(ref, hold_ref.at[i], sems.at[i]))
        stores.append(pltpu.make_async_copy(hold_ref.at[i], part, sems.at[2 + i]))
    for c in loads:
        c.start()
    for load, store in zip(loads, stores):
        load.wait()
        store.start()
    for c in stores:
        c.wait()


def join(first, second):
    anywhere = pl.BlockSpec(memory_space=pl.ANY)
    n, rows, width = first.shape
    return pl.pallas_call(
        join_kernel,
        in_specs=[anywhere] * 2,
        out_specs=anywhere,
        out_shape=jax.ShapeDtypeStruct((n, 2 * rows, width), first.dtype),
        scratch_shapes=[
            pltpu.VMEM((2, n, rows, width), first.dtype),
            pltpu.SemaphoreType.DMA((4,)),
        ],
        compiler_params=pltpu.CompilerParams(vmem_limit_bytes=56 << 20),
        cost_estimate=pl.CostEstimate(
            flops=0, bytes_accessed=8 * first.size, transcendentals=0
        ),
        name="join",
    )(first, second)


def after(x, *earlier):
    return lax.optimization_barrier((x, *earlier))[0]


def exchange(x, axis):
    return lax.all_to_all(x, axis, split_axis=0, concat_axis=0, tiled=True)


def per_device(tokens, expert_ids, router_weights, partner, gate_up, down):
    n_tok, feature = tokens.shape
    units = gate_up.shape[3]
    yh = lax.axis_index("yh")
    yl = lax.axis_index("yl")
    base = (yl * 8 + yh).astype(jnp.int32).reshape(1)

    mine = yh.astype(jnp.int32).reshape(1)
    give_up, give_down = gate_up[-1], down[-1]
    mine = after(mine, give_up)
    own_up, other_up = cut(mine, gate_up)
    own_down, other_down = cut(mine, down)

    norm = router_weights / jnp.sum(router_weights, axis=1, keepdims=True)
    high = lax.reduce_precision(norm, 8, 7)
    meta = jnp.concatenate(
        [expert_ids.astype(F32), high, norm - high, jnp.zeros((n_tok, 104), F32)], axis=1
    )
    packed = jnp.concatenate([tokens, meta.astype(BF)], axis=1)
    packed = after(packed, give_up)
    blocks = [packed] + [lax.ppermute(packed, COLUMN, along_y(k)) for k in (1, 3, 2)]
    slot, weight, placed = placement(base, blocks, feature)

    near_up = exchange(give_up.reshape(N_PLANE, -1, units), PLANE)
    side_up = lax.ppermute(own_up, "c", SWAP)
    side_down = lax.ppermute(own_down, "c", SWAP)
    far_up = lax.ppermute(after(other_up, *blocks[1:]), "yh", SWAP)
    outgoing = dispatch(placed, blocks, feature)
    outgoing = after(outgoing, near_up, other_down, own_down)
    arrived = exchange(outgoing.reshape(N_PLANE, N_COL * CAP, feature), PLANE)
    x = arrived.reshape(N_PLANE * N_COL * CAP, feature)
    half = near_up.shape[1] // 2
    near_gate, near_rest = near_up[:, :half], near_up[:, half:]
    far_down = lax.ppermute(after(other_down, far_up), "yh", SWAP)
    far_side_up = lax.ppermute(far_up, "c", SWAP)
    hidden = hidden_all(after(x, near_gate, near_rest), (own_up, side_up, far_up, far_side_up))
    near_down = exchange(after(give_down, arrived).reshape(N_PLANE, -1, feature), PLANE)
    far_down = after(far_down, hidden, near_down)
    far_side_down = lax.ppermute(far_down, "c", SWAP)
    y = down_all(hidden, (own_down, side_down, far_down, far_side_down))
    back = exchange(y.reshape(N_PLANE, N_COL * CAP, feature), PLANE)
    parts = combine(slot, weight, back.reshape(N_PLANE * N_COL * CAP, feature))
    from_host = lax.dynamic_index_in_dim(partner.reshape(4, 2, 4), yl, 1, keepdims=False)
    from_host = from_host.T.reshape(-1)
    crossed = (from_host // 4) % 2 != yl
    source = (from_host % 4) * 4 + from_host // 8 + jnp.where(crossed, N_PLANE, 0)
    source = source.astype(jnp.int32)
    nears = (near_gate, near_rest, near_down)
    crossed, last = [], far_down
    for near in nears:
        last = lax.ppermute(after(near, last), "yl", SWAP)
        crossed.append(last)
    landed = [back]
    for i, near in enumerate(nears):
        at = after(source, *(() if i < 2 else parts))
        forward = pick(at, near, crossed[i])
        landed.append(exchange(after(forward, landed[-1]), PLANE))
    landed_up, landed_down = join(landed[1], landed[2]), landed[3]

    mixed = after(parts[0], landed_up)
    for part, k in zip(parts[1:], (3, 1, 2)):
        mixed = mixed + lax.ppermute(part, COLUMN, along_y(k)).astype(F32)
    mixed = mixed.astype(BF)
    return (
        mixed,
        landed_up.reshape((1,) + gate_up.shape[1:]),
        landed_down.reshape((1,) + down.shape[1:]),
    )


def solution(mesh):
    fine = Mesh(np.asarray(mesh.devices).reshape(4, 2, 4, 2, 2), ("z", "yl", "x", "yh", "c"))
    dp = ("yh", "c")
    rows = P(HOST + dp, None)
    up = P(HOST, None, None, dp)
    out = P(HOST, dp, None)
    return jax.shard_map(
        per_device,
        mesh=fine,
        in_specs=(rows, rows, rows, P(), up, out),
        out_specs=(rows, up, out),
        check_vma=False,
    )
```
